32 devices in a mesh: narrow: 4 (over y, x), region: 8 (over z, core).
Axes of the slice: x: 2, y: 2, z: 4, core: 2. Of those that a mesh axis runs over, the one named last changes fastest.
Arguments:
- point_feats: bfloat16 [64, 131072], P(None, ('narrow', 'region')), may hold values from -6 to 6
- point_owner: int32 [131072, 1], P(('narrow', 'region')), may hold values from 0 to 31; in each aligned block of 4096 rows (0 to 4095, 4096 to 8191, ...) at most 256 rows name the same one
- point_voxel: int32 [131072], P(('narrow', 'region')), may hold values from 0 to 12287
- weight: bfloat16 [9, 64, 192], replicated, may hold values from -0.15625 to 0.15625
- cotangent: bfloat16 [64, 192, 2048], P(None, 'region', 'narrow'), may hold values from -6 to 6
Outputs:
- conv_out: bfloat16 [64, 192, 2048], P(None, 'region', 'narrow')
- point_grad: bfloat16 [64, 131072], P(None, ('narrow', 'region'))
- weight_grad: float32 [9, 64, 192], replicated
The draws below stay inside these ranges and needn't reach their ends.
Inputs may be any that keep to these rules, and one draw needn't show every extreme that they name: `point_owner`: among the 4096 points of one device no owner is named more than 256 times, a bound that some block reaches.
All inputs are finite; a program needn't handle non-finite values.
Results may differ from the reference program's by a relative error of at most 0.0036.
Values may be sent and summed in bfloat16 or wider, within the bound.
A program may use at most 192 MiB of HBM per device.

```python
import math
import jax
import jax.numpy as jnp
import numpy as np
from jax import lax

C = 64
NZ = 64
CY = 8
CX = 24
P_DEV = 4096
CAP = 256
VOX_DEV = 12288
NX = 192
NY = 32
POINTS = 131072
N_REGION = 8
DEVICES = 32


def with_ends(drawn, own_key, least, top_value):
    index_at = [jax.random.randint(jax.random.fold_in(own_key, axis), (), 0, length) for axis, length in enumerate(drawn.shape)]
    main_axis = drawn.shape.index(max(drawn.shape))
    beside = index_at[:main_axis] + [(index_at[main_axis] + 1) % drawn.shape[main_axis]] + index_at[main_axis + 1:]
    return drawn.at[tuple(index_at)].set(least).at[tuple(beside)].set(top_value)


def levels(rng, dims, split, low, largest):
    gain, own = 1.0, jax.random.fold_in(rng, 6)
    for position, shards_of in split:
        heights = jnp.exp(jax.random.uniform(jax.random.fold_in(own, position), (shards_of,), jnp.float32, low / len(split), largest / len(split)))
        gain = gain * jnp.repeat(heights, dims[position] // shards_of).reshape([-1 if axis == position else 1 for axis in range(len(dims))])
    return gain


def deal_out(key, own, number, rows, count, top, bound, slope):
    order = jax.random.permutation(key, count)
    heavy_load, usual = load_shares(count, rows * top, bound, slope, True), load_shares(count, rows * top, bound, slope, False)
    places = jnp.arange(count)

    def named(tallies, offset_by):
        used = int((tallies > 0).sum())
        fixed = max(1, used // 4)
        passed = fixed + (places - fixed + offset_by * (used - fixed)) % max(1, count - fixed)
        return jnp.zeros((count,), jnp.int32).at[order[jnp.where(places < fixed, places, passed)]].set(jnp.asarray(tallies, jnp.int32))

    tallies = jnp.where(number % 4 == 0, named(heavy_load, number // 4), named(usual, number - number // 4 - 1))
    mixed = jax.random.permutation(jax.random.fold_in(own, 3), count)
    giver, sink = mixed[0:count // 2 * 2:2], mixed[1:count // 2 * 2:2]
    slack = jnp.minimum(tallies[giver] - 1, bound - tallies[sink]) // 2
    slack = jnp.where((giver == order[0]) | (sink == order[0]) | (tallies[sink] == 0), 0, jnp.maximum(slack, 0))
    passed = jax.random.randint(jax.random.fold_in(own, 4), (count // 2,), 0, 1 << 20) % (slack + 1)
    tallies = tallies.at[giver].add(-passed).at[sink].add(passed)
    members = jnp.searchsorted(jnp.cumsum(tallies), jnp.arange(rows * top), side="right").astype(jnp.int32)
    listing = members.reshape(top, rows).T
    listing = listing[jax.random.permutation(jax.random.fold_in(own, 1), rows)]
    offset_by = jax.random.randint(jax.random.fold_in(own, 2), (rows, 1), 0, top)
    return jnp.take_along_axis(listing, (jnp.arange(top)[None, :] + offset_by) % top, axis=1)


def load_shares(amount, total, bound, skew, full):
    portions = [(1 << 20) // math.isqrt(grade ** skew) + 1 for grade in range(1, amount + 1)]
    largest = bound if full else min(bound, max(-(-total // amount), total * portions[0] // sum(portions)))
    least = 1 if total - largest >= amount - 1 else 0
    holding, surplus = [largest] + [least] * (amount - 1), total - largest - least * (amount - 1)
    while surplus > 0:
        movable = [i for i in range(1, amount) if holding[i] < largest] or [i for i in range(1, amount) if holding[i] < bound]
        pool, budget = sum([portions[i] for i in movable]), surplus
        for i in movable:
            addition = min(bound - holding[i], max(1, budget * portions[i] // pool), surplus)
            holding[i] = holding[i] + addition
            surplus = surplus - addition
    return np.array(holding)


def bell_draw(stream_key, dims, deviation, bound, pieces=(), held_as=jnp.bfloat16):
    values = jax.random.normal(stream_key, dims, jnp.float32) * deviation
    if len(pieces) > 0:
        values = levels(stream_key, dims, pieces, -0.22, 0.18) * values
    return jnp.clip(values, min=-bound, max=bound).astype(held_as)


def setup_inputs(seed: int = 0) -> dict:
    keys = jax.random.split(jax.random.key(seed), 6)
    point_feats = bell_draw(keys[0], (C, POINTS), 1.0, 6.0, ((1, 32),))
    point_owner_keys = jax.random.split(jax.random.fold_in(keys[1], 1), POINTS // P_DEV)
    point_owner_turns = jax.random.permutation(jax.random.fold_in(keys[1], 3), POINTS // P_DEV)
    point_owner = jax.vmap(lambda own, number: deal_out(jax.random.fold_in(keys[1], 2), own, number, P_DEV, DEVICES, 1, CAP, 2))(point_owner_keys, point_owner_turns).reshape((POINTS, 1))
    point_voxel = with_ends(jax.random.randint(keys[2], (POINTS,), 0, VOX_DEV), jax.random.fold_in(keys[2], 1), 0, VOX_DEV - 1).astype(jnp.int32)
    weight = bell_draw(keys[3], (9, C, 3 * C), (27 * C) ** -0.5, 0.15625)
    cotangent = bell_draw(keys[4], (C, NX, NY * NZ), 1.0, 6.0, ((1, 8), (2, 4)))
    return dict(point_feats=point_feats, point_owner=point_owner, point_voxel=point_voxel, weight=weight, cotangent=cotangent)


def stack_depth(padded, offsets, depth):
    return jnp.concatenate([padded[..., o:o + depth] for o in offsets], axis=0)

def reference(point_feats, point_owner, point_voxel, weight, cotangent):
    owner = point_owner[:, 0]
    narrow_idx = owner // N_REGION
    region_idx = owner % N_REGION
    local_x = point_voxel // (CY * NZ)
    local_y = point_voxel // NZ % CY
    local_z = point_voxel % NZ
    flat = (((region_idx * CX + local_x) * NY + narrow_idx * CY + local_y) * NZ + local_z).astype(jnp.int32)
    sums = jax.ops.segment_sum(point_feats.astype(jnp.float32).T, flat, num_segments=NX * NY * NZ)
    grid = sums.T.astype(jnp.bfloat16).reshape(C, NX, NY, NZ)
    padded = jnp.pad(grid, ((0, 0), (1, 1), (1, 1), (1, 1)))
    stacked = stack_depth(padded, [0, 1, 2], NZ)
    grads = cotangent.reshape(C, NX, NY, NZ)
    gpad = jnp.pad(grads, ((0, 0), (1, 1), (1, 1), (1, 1)))
    gstack = stack_depth(gpad, [2, 1, 0], NZ)
    flipped = weight.reshape(9, C, 3, C).transpose(0, 3, 2, 1).reshape(9, C, 3 * C)

    def slab(index):
        start = (index * CX).astype(jnp.int32)
        xs = lax.dynamic_slice_in_dim(stacked, start, CX + 2, 1).astype(jnp.float32)
        gs = lax.dynamic_slice_in_dim(gstack, start, CX + 2, 1).astype(jnp.float32)
        gl = lax.dynamic_slice_in_dim(grads, start, CX, 1).astype(jnp.float32)
        result = jnp.zeros((C, CX, NY, NZ), jnp.float32)
        backward = jnp.zeros((C, CX, NY, NZ), jnp.float32)
        kernels = []
        for a in range(3):
            for b in range(3):
                k = a * 3 + b
                window = xs[:, a:a + CX, b:b + NY]
                result = result + jnp.einsum('ok,kxyz->oxyz', weight[k].astype(jnp.float32), window)
                kernels.append(jnp.einsum('oxyz,kxyz->ok', gl, window))
                backward = backward + jnp.einsum('ck,kxyz->cxyz', flipped[k].astype(jnp.float32), gs[:, 2 - a:2 - a + CX, 2 - b:2 - b + NY])
        return (result, backward, jnp.stack(kernels))
    results, backwards, kernels = lax.map(slab, jnp.arange(N_REGION, dtype=jnp.int32))
    conv_out = results.transpose(1, 0, 2, 3, 4).reshape(C, NX, NY * NZ).astype(jnp.bfloat16)
    grad_grid = backwards.transpose(1, 0, 2, 3, 4).reshape(C, NX * NY * NZ).astype(jnp.bfloat16)
    point_grad = jnp.take(grad_grid, flat, axis=1)
    weight_grad = lax.optimization_barrier(jnp.sum(kernels, axis=0)) * (1.0 / math.sqrt(NX * NY * NZ))
    return (conv_out, point_grad, weight_grad)
```

```python
import functools
import math

import jax
import jax.numpy as jnp
from jax import lax
from jax.experimental import pallas as pl
from jax.experimental.pallas import tpu as pltpu
from jax.sharding import PartitionSpec as P

NZ = 64
CY = 8
AXES = ("narrow", "region")
GROUP = 8
TILE = 512


def halos(grid, n_narrow, n_region):
    rows_x, _, depth, chans = grid.shape
    half = depth // 2

    def paired(cells):
        return jnp.concatenate([cells[..., :half, :], cells[..., half:, :]], axis=-1)

    def sent(cells, dn, dr):
        pairs = [
            (n * n_region + r, (n + dn) * n_region + r + dr)
            for n in range(n_narrow)
            for r in range(n_region)
            if 0 <= n + dn < n_narrow and 0 <= r + dr < n_region
        ]
        return lax.ppermute(cells, AXES, pairs)

    left, right = sent(paired(grid[:, CY - 1]), 1, 0), sent(paired(grid[:, 0]), -1, 0)
    top, bottom = sent(paired(grid[rows_x - 1]), 0, 1), sent(paired(grid[0]), 0, -1)
    far_left = sent(jnp.stack([top[CY - 1], bottom[CY - 1]]), 1, 0)
    far_right = sent(jnp.stack([top[0], bottom[0]]), -1, 0)
    top = jnp.concatenate([far_left[:1], top, far_right[:1]])
    bottom = jnp.concatenate([far_left[1:], bottom, far_right[1:]])
    return left, right, top, bottom


def stack_kernel(inside_ref, center, *refs):
    far, (out, left, right, top, bottom, arrived) = refs[:4], refs[-6:]
    copies = [
        pltpu.make_async_copy(source, target, arrived.at[i])
        for i, (source, target) in enumerate(zip(far, (left, right, top, bottom)))
    ]
    for copy in copies:
        copy.start()
    rows_x, _, depth, chans = center.shape
    f32 = jnp.float32
    row = lax.broadcasted_iota(jnp.int32, (depth, chans), 0)
    west, east, north, south = [inside_ref[i] for i in range(4)]

    def spread(tile, keep=None):
        t = tile.astype(f32)
        if keep is not None:
            t = jnp.concatenate([t[:, :chans], t[:, chans:]], axis=0)
            t = jnp.where(keep > 0, t, 0.0)
        up = jnp.where(row == 0, 0.0, pltpu.roll(t, 1, 0))
        down = jnp.where(row == depth - 1, 0.0, pltpu.roll(t, depth - 1, 0))
        return jnp.concatenate([up, t, down], axis=1).astype(jnp.bfloat16)

    def plane(x, _):
        for y in range(CY):
            out[x + 1, y + 1] = spread(center[x, y])

    def sides(x, _):
        out[x + 1, 0] = spread(left[x], west)
        out[x + 1, CY + 1] = spread(right[x], east)

    lax.fori_loop(0, rows_x, plane, None)
    for copy in copies:
        copy.wait()
    lax.fori_loop(0, rows_x, sides, None)
    for at, end, keep in ((0, top, north), (rows_x + 1, bottom, south)):
        out[at, 0] = spread(end[0], keep * west)
        out[at, CY + 1] = spread(end[CY + 1], keep * east)
        for y in range(1, CY + 1):
            out[at, y] = spread(end[y], keep)


def stack_weight_kernel(inside_ref, center, left, right, top, bottom, flat, out, sums, *scratch):
    stack_kernel(inside_ref, center, left, right, top, bottom, out, *scratch)
    sums[...] = jnp.zeros_like(sums)
    plane_cells = CY * NZ

    def plane(x, _):
        here = flat[:, pl.ds(pl.multiple_of(x * plane_cells, plane_cells), plane_cells)]
        for a in range(3):
            for b in range(3):
                window = out[x + a, b : b + CY].reshape(plane_cells, out.shape[3])
                sums[3 * a + b] += jnp.dot(here, window, preferred_element_type=jnp.float32)

    lax.fori_loop(0, center.shape[0], plane, None)


def stacked_depth(cells, edges, n_narrow, n_region, flat=None):
    rows_x, _, depth, chans = cells.shape
    n, r = lax.axis_index("narrow"), lax.axis_index("region")
    inside = jnp.stack([n > 0, n < n_narrow - 1, r > 0, r < n_region - 1]).astype(jnp.int32)
    stack = jax.ShapeDtypeStruct((rows_x + 2, CY + 2, depth, 3 * chans), cells.dtype)
    scratch = [pltpu.VMEM(e.shape, e.dtype) for e in edges] + [pltpu.SemaphoreType.DMA((4,))]
    if flat is None:
        return call(stack_kernel, stack, "svaaaa", "v", scratch, 40 << 20, inside, cells, *edges)
    sums = jax.ShapeDtypeStruct((9, chans, 3 * chans), jnp.float32)
    return call(
        stack_weight_kernel,
        (stack, sums),
        "svaaaav",
        "vv",
        scratch,
        80 << 20,
        inside,
        cells,
        *edges,
        flat,
    )


def convolved(stack, kernel):
    return lax.conv_general_dilated(
        stack,
        kernel,
        (1, 1),
        "VALID",
        dimension_numbers=lax.ConvDimensionNumbers((2, 3, 0, 1), (3, 2, 0, 1), (2, 3, 0, 1)),
        preferred_element_type=jnp.float32,
    )


def packed(buf, out_ref, half):
    devices = out_ref.shape[0]

    def block(s, _):
        low = pl.multiple_of(s * half, half)
        left = buf[pl.ds(low, half), :]
        right = buf[pl.ds(devices * half + low, half), :]
        out_ref[s, pl.ds(0, half), :] = jnp.concatenate([left, right], axis=1).astype(jnp.bfloat16)

    lax.fori_loop(0, devices, block, None)


def unpacked(in_ref, buf, half):
    devices, _, lanes = in_ref.shape

    def block(s, _):
        low = pl.multiple_of(s * half, half)
        both = in_ref[s, pl.ds(0, half), :].astype(jnp.float32)
        buf[pl.ds(low, half), :] = both[:, : lanes // 2]
        buf[pl.ds(devices * half + low, half), :] = both[:, lanes // 2 :]

    lax.fori_loop(0, devices, block, None)


def each_arrival(devices, slots, count_ref, visit):
    half = slots // 2
    rows = devices * half

    def source(s, _):
        here = count_ref[s]
        for h in range(2):
            some = jnp.clip(here - h * half, 0, half)

            def group(j, _):
                for u in range(GROUP):
                    r = j * GROUP + u
                    visit(u, s * slots + h * half + r, h * rows + s * half + r)

            lax.fori_loop(0, (some + GROUP - 1) // GROUP, group, None)

    lax.fori_loop(0, devices, source, None)


def place_kernel(half, place_ref, vox_ref, rows_ref, out_ref, vox_out_ref, buf):
    def group(j, _):
        for u in range(GROUP):
            p = j * GROUP + u
            d = place_ref[p]
            buf[pl.ds(d, 1), :] = rows_ref[pl.ds(p, 1), :]
            vox_out_ref[d] = vox_ref[p]

    lax.fori_loop(0, rows_ref.shape[0] // GROUP, group, None)
    packed(buf, out_ref, half)


def splat_kernel(devices, slots, vox_ref, count_ref, got_ref, grid_ref, buf, *sums):
    unpacked(got_ref, buf, slots // 2)
    voxels, chans = grid_ref.shape

    def clear(t, _):
        for each in sums:
            each[pl.ds(pl.multiple_of(t * TILE, TILE), TILE), :] = jnp.zeros((TILE, chans), jnp.float32)

    lax.fori_loop(0, voxels // TILE, clear, None)

    def visit(u, k, r):
        v = vox_ref[k]
        each = sums[u % len(sums)]
        each[pl.ds(v, 1), :] += buf[pl.ds(r, 1), :]

    each_arrival(devices, slots, count_ref, visit)

    def finish(t, _):
        at = pl.ds(pl.multiple_of(t * TILE, TILE), TILE)
        total = sums[0][at, :]
        for each in sums[1:]:
            total += each[at, :]
        grid_ref[at, :] = total.astype(jnp.bfloat16)

    lax.fori_loop(0, voxels // TILE, finish, None)


def pick_kernel(devices, slots, vox_ref, count_ref, table_ref, out_ref, buf):
    def visit(u, k, r):
        buf[pl.ds(r, 1), :] = table_ref[pl.ds(vox_ref[k], 1), :]

    each_arrival(devices, slots, count_ref, visit)
    packed(buf, out_ref, slots // 2)


def collect_kernel(half, place_ref, back_ref, out_ref, buf):
    unpacked(back_ref, buf, half)

    def group(j, _):
        for u in range(GROUP):
            p = j * GROUP + u
            out_ref[pl.ds(p, 1), :] = buf[pl.ds(place_ref[p], 1), :]

    lax.fori_loop(0, out_ref.shape[0] // GROUP, group, None)


def call(kernel, out_shape, kinds, out_kinds, scratch, cost, *operands):
    where = {"s": pltpu.SMEM, "v": pltpu.VMEM, "a": pl.ANY}
    specs = [pl.BlockSpec(memory_space=where[k]) for k in out_kinds]
    return pl.pallas_call(
        kernel,
        out_shape=out_shape,
        in_specs=[pl.BlockSpec(memory_space=where[k]) for k in kinds],
        out_specs=specs if len(specs) > 1 else specs[0],
        scratch_shapes=scratch,
        compiler_params=pltpu.CompilerParams(vmem_limit_bytes=50 << 20),
        cost_estimate=pl.CostEstimate(flops=0, bytes_accessed=cost, transcendentals=0),
    )(*operands)


def ranks(owner, devices):
    span = 128
    chunks = owner.shape[0] // span
    marks = owner.reshape(chunks, span)[:, :, None] == jnp.arange(devices, dtype=jnp.int32)
    ones = marks.astype(jnp.bfloat16)
    before = (jnp.arange(span)[:, None] > jnp.arange(span)[None, :]).astype(jnp.bfloat16)
    inner = jnp.einsum("ij,cjo->cio", before, ones, preferred_element_type=jnp.float32)
    tallies = jnp.sum(ones.astype(jnp.float32), axis=1)
    ahead = (jnp.arange(chunks)[:, None] > jnp.arange(chunks)[None, :]).astype(jnp.bfloat16)
    starts = jnp.einsum("ij,jo->io", ahead, tallies.astype(jnp.bfloat16), preferred_element_type=jnp.float32)
    slot = jnp.sum(jnp.where(marks, inner + starts[:, None, :], 0.0), axis=2)
    return slot.reshape(-1).astype(jnp.int32), jnp.sum(tallies, axis=0).astype(jnp.int32)


def exchanged(x):
    return lax.all_to_all(x, AXES, split_axis=0, concat_axis=0, tiled=True)


def shards(point_feats, point_owner, point_voxel, weight, cotangent):
    n_narrow = lax.axis_size("narrow")
    n_region = lax.axis_size("region")
    devices = n_narrow * n_region
    chans, points_here = point_feats.shape
    slots = 2 * points_here // devices
    half = slots // 2
    rows = devices * half
    rows_x = cotangent.shape[1]
    voxels = rows_x * CY * NZ
    f32, bf16, i32 = jnp.float32, jnp.bfloat16, jnp.int32
    buffer = pltpu.VMEM((2 * rows, chans), f32)
    pairs = jax.ShapeDtypeStruct((devices, half, 2 * chans), bf16)
    spare = 16
    block = jax.ShapeDtypeStruct((devices, half + spare, 2 * chans), bf16)

    grads = cotangent.reshape(chans, rows_x, CY, NZ).transpose(1, 2, 3, 0)
    grad_edges = halos(grads, n_narrow, n_region)

    owner = point_owner[:, 0]
    slot, sent = ranks(owner, devices)
    place = (slot // half) * rows + owner * half + slot % half
    send, send_vox = call(
        functools.partial(place_kernel, half),
        (block, jax.ShapeDtypeStruct((2 * rows,), i32)),
        "ssv",
        "vs",
        [buffer],
        40 << 20,
        place,
        point_voxel,
        point_feats.T.astype(f32),
    )
    send_vox = send_vox.reshape(2, devices, half).transpose(1, 0, 2).reshape(devices, slots)
    filled = jnp.arange(slots, dtype=i32)[None, :] < sent[:, None]
    send_vox = jnp.where(filled, send_vox, voxels)
    digits = jnp.concatenate([send_vox // 128, send_vox % 128], axis=1).astype(bf16)
    digits = jnp.pad(digits, ((0, 0), (0, spare * 2 * chans - 2 * slots)))
    digits = digits.reshape(devices, spare, 2 * chans)
    got = exchanged(lax.dynamic_update_slice(send, digits, (0, half, 0)))
    digits = got[:, half:].reshape(devices, spare * 2 * chans).astype(i32)
    got_vox = digits[:, :slots] * 128 + digits[:, slots : 2 * slots]
    count = jnp.sum((got_vox < voxels).astype(i32), axis=1)
    add_at = got_vox.reshape(-1)
    pick_at = jnp.where(got_vox < voxels, got_vox, 0).reshape(-1)

    w = weight.reshape(3, 3, chans, 3, chans)
    backward = w[::-1, ::-1, :, ::-1, :].transpose(0, 1, 3, 2, 4).reshape(3, 3, 3 * chans, chans)
    forward = weight.reshape(3, 3, chans, 3 * chans).transpose(0, 1, 3, 2)

    grad_stack = stacked_depth(grads, grad_edges, n_narrow, n_region)
    table = convolved(grad_stack, backward).reshape(voxels, chans)
    picked = call(
        functools.partial(pick_kernel, devices, slots),
        pairs,
        "ssv",
        "v",
        [buffer],
        40 << 20,
        pick_at,
        count,
        table,
    )
    picked, got = lax.optimization_barrier((picked, got))
    back = exchanged(picked)

    grid = call(
        functools.partial(splat_kernel, devices, slots),
        jax.ShapeDtypeStruct((voxels, chans), bf16),
        "ssv",
        "v",
        [buffer] + [pltpu.VMEM((voxels + 8, chans), f32)] * 4,
        80 << 20,
        add_at,
        count,
        got,
    )
    cells = grid.reshape(rows_x, CY, NZ, chans)
    cell_edges = halos(cells, n_narrow, n_region)
    back, cells = lax.optimization_barrier((back, cells))
    point_rows = call(
        functools.partial(collect_kernel, half),
        jax.ShapeDtypeStruct((points_here, chans), f32),
        "sv",
        "v",
        [buffer],
        20 << 20,
        place,
        back,
    )
    point_rows, cells = lax.optimization_barrier((point_rows, cells))
    flat = cotangent.reshape(chans, voxels)
    stack, kernels = stacked_depth(cells, cell_edges, n_narrow, n_region, flat)
    total_cells = rows_x * n_region * CY * n_narrow * NZ
    parts = exchanged(kernels.reshape(devices, -1))
    mine = jnp.sum(parts, axis=0) * (1.0 / math.sqrt(total_cells))
    everywhere = exchanged(jnp.broadcast_to(mine, (devices, mine.shape[0])))
    weight_grad = everywhere.reshape(9, chans, 3 * chans)

    result = convolved(stack, forward).astype(bf16)
    conv_out = result.transpose(3, 0, 1, 2).reshape(chans, rows_x, CY * NZ)

    return (conv_out, point_rows.T.astype(bf16), weight_grad)


def solution(mesh):
    in_specs = (
        P(None, AXES),
        P(AXES, None),
        P(AXES),
        P(),
        P(None, "region", "narrow"),
    )
    out_specs = (P(None, "region", "narrow"), P(None, AXES), P())
    return jax.shard_map(shards, mesh=mesh, in_specs=in_specs, out_specs=out_specs, check_vma=False)
```

```python
import functools
import math

import jax
import jax.numpy as jnp
from jax import lax
from jax.experimental import pallas as pl
from jax.experimental.pallas import tpu as pltpu
from jax.sharding import PartitionSpec as P

NZ = 64
CY = 8
AXES = ("narrow", "region")
GROUP = 8
UNROLL = 16
TILE = 512
PAIRS = CY // 2 + 1
MESH = pl.DeviceIdType.MESH


def dot(a, b):
    return jnp.dot(a, b, preferred_element_type=jnp.float32)


def low_lanes(rows):
    return lax.broadcasted_iota(jnp.int32, (rows, 128), 1) < 64


def swapped(t):
    return pltpu.roll(t, 64, 1)


def device(flat, n_region):
    return (flat // n_region, lax.rem(flat, n_region))


def meet_all(devices, n_region, me):
    barrier = pltpu.get_barrier_semaphore()

    def greet(s, _):
        other = device(lax.rem(me + s, devices), n_region)
        pl.semaphore_signal(barrier, inc=1, device_id=other, device_id_type=MESH)

    lax.fori_loop(1, devices, greet, None)
    pl.semaphore_wait(barrier, devices - 1)


def halo_moves(n_narrow, n_region, center, faces, left, right, top, bottom, corners, send, recv):
    n, r = lax.axis_index("narrow"), lax.axis_index("region")
    last = center.shape[0] - 1
    west, east = lax.rem(n + n_narrow - 1, n_narrow), lax.rem(n + 1, n_narrow)
    north, south = lax.rem(r + n_region - 1, n_region), lax.rem(r + 1, n_region)
    w, e, u, d = n > 0, n < n_narrow - 1, r > 0, r < n_region - 1
    both = jnp.logical_and
    table = [
        (w, e, (west, r), faces.at[0], right),
        (e, w, (east, r), faces.at[1], left),
        (u, d, (n, north), center.at[0], bottom),
        (d, u, (n, south), center.at[last], top),
        (both(w, u), both(e, d), (west, north), center.at[0, 0], corners.at[3]),
        (both(e, u), both(w, d), (east, north), center.at[0, PAIRS - 1], corners.at[2]),
        (both(w, d), both(e, u), (west, south), center.at[last, 0], corners.at[1]),
        (both(e, d), both(w, u), (east, south), center.at[last, PAIRS - 1], corners.at[0]),
    ]
    return [
        (
            sends,
            gets,
            pltpu.make_async_remote_copy(
                src_ref=source,
                dst_ref=target,
                send_sem=send.at[i],
                recv_sem=recv.at[i],
                device_id=where,
                device_id_type=MESH,
            ),
            target,
        )
        for i, (sends, gets, where, source, target) in enumerate(table)
    ]


def start_halo(moves, center, faces):
    half_x = center.shape[0] // 2
    f32 = jnp.float32

    def face(x, _):
        for i, k in ((0, 0), (1, PAIRS - 1)):
            tile = center[x, k].astype(f32) + swapped(center[x + half_x, k].astype(f32))
            faces[i, x] = tile.astype(jnp.bfloat16)

    lax.fori_loop(0, half_x, face, None)
    for sends, gets, copy, target in moves:

        @pl.when(sends)
        def _():
            copy.start()

        @pl.when(jnp.logical_not(gets))
        def _():
            target[...] = jnp.zeros(target.shape, target.dtype)


def wait_halo(moves):
    for sends, gets, copy, _ in moves:

        @pl.when(gets)
        def _():
            copy.wait_recv()

        @pl.when(sends)
        def _():
            copy.wait_send()


def put(stack, x, k, t):
    row = lax.broadcasted_iota(jnp.int32, t.shape, 0)
    at = pl.ds(k * NZ, NZ)
    up = jnp.where(row == 0, 0.0, pltpu.roll(t, 1, 0))
    down = jnp.where(row == NZ - 1, 0.0, pltpu.roll(t, NZ - 1, 0))
    stack[x, 0, at, :] = up.astype(jnp.bfloat16)
    stack[x, 1, at, :] = t.astype(jnp.bfloat16)
    stack[x, 2, at, :] = down.astype(jnp.bfloat16)


def stack_inside(stack, center):
    def plane(x, _):
        for k in range(1, PAIRS - 1):
            put(stack, x + 1, k, center[x, k].astype(jnp.float32))

    lax.fori_loop(0, center.shape[0], plane, None)


def stack_edges(stack, center, left, right, top, bottom, corners):
    rows_x = center.shape[0]
    half_x = rows_x // 2
    f32 = jnp.float32
    low = low_lanes(NZ)
    end = PAIRS - 1

    def sides(x, _):
        from_left, from_right = left[x].astype(f32), right[x].astype(f32)
        for at, l, r in (
            (x, from_left, from_right),
            (x + half_x, swapped(from_left), swapped(from_right)),
        ):
            put(stack, at + 1, 0, center[at, 0].astype(f32) + jnp.where(low, l, 0.0))
            put(stack, at + 1, end, center[at, end].astype(f32) + jnp.where(low, 0.0, r))

    lax.fori_loop(0, half_x, sides, None)
    for x, rows, c in ((0, top, 0), (rows_x + 1, bottom, 2)):
        for k in range(PAIRS):
            t = rows[k].astype(f32)
            if k == 0:
                t += corners[c].astype(f32)
            if k == end:
                t += corners[c + 1].astype(f32)
            put(stack, x, k, t)


def window(stack, x, d):
    rows = (PAIRS - 1) * NZ
    return jnp.concatenate([stack[x, d, pl.ds(0, rows), :], stack[x, d, pl.ds(NZ, rows), :]], axis=1)


def convolve(stack, w, emit):
    def step(xp, _):
        total = None
        for i in range(4):
            for d in range(3):
                term = dot(window(stack, 2 * xp + i, d), w[3 * i + d])
                total = term if total is None else total + term
        emit(xp, total)

    lax.fori_loop(0, (stack.shape[0] - 2) // 2, step, None)


def to_each(devices, n_region, me, source, target, send, recv, visit):
    def copy(s):
        other = lax.rem(me + s, devices)
        return pltpu.make_async_remote_copy(
            src_ref=source(other),
            dst_ref=target,
            send_sem=send.at[s],
            recv_sem=recv.at[s],
            device_id=device(other, n_region),
            device_id_type=MESH,
        )

    def go(s, _):
        visit(lax.rem(me + s, devices))
        copy(s).start()

    def finish(s, _):
        copy(s).wait_recv()
        copy(s).wait_send()

    lax.fori_loop(1, devices, go, None)
    return lambda: lax.fori_loop(1, devices, finish, None)


def paired_rows(first, second, table, base, rows, buf):
    low = low_lanes(1)

    def group(j, _):
        for u in range(UNROLL):
            q = j * UNROLL + u
            a = table[pl.ds(first[base + q], 1), :]
            b = table[pl.ds(second[base + q], 1), :]
            buf[pl.ds(q, 1), :] = jnp.where(low, a, b)

    lax.fori_loop(0, rows // UNROLL, group, None)


def outward_kernel(
    n_narrow, n_region, first, second, feats, digits, center, w,
    got, table,
    block, buf, faces, left, right, top, bottom, corners, stack,
    send, recv, halo_send, halo_recv,
):
    devices = n_narrow * n_region
    me = lax.axis_index("narrow") * n_region + lax.axis_index("region")
    half = buf.shape[0]
    spare = digits.shape[1]
    meet_all(devices, n_region, me)
    moves = halo_moves(
        n_narrow, n_region, center, faces, left, right, top, bottom, corners, halo_send, halo_recv
    )
    start_halo(moves, center, faces)

    def fill(ref, at, other):
        paired_rows(first, second, feats, other * half, half, buf)
        ref[at, pl.ds(0, half), :] = buf[...].astype(jnp.bfloat16)
        ref[at, pl.ds(half, spare), :] = digits[other]

    arrive = to_each(
        devices, n_region, me, lambda o: block.at[o], got.at[me], send, recv, lambda o: fill(block, o, o)
    )
    fill(got, me, me)
    stack_inside(stack, center)
    wait_halo(moves)
    stack_edges(stack, center, left, right, top, bottom, corners)
    rows = (PAIRS - 1) * NZ

    def emit(xp, total):
        for i in range(2):
            at = pl.multiple_of((2 * xp + i) * rows, rows)
            table[pl.ds(at, rows), :] = total[:, i * 128 : (i + 1) * 128]

    convolve(stack, w, emit)
    arrive()


def splat_kernel(devices, slots, vox_ref, count_ref, got_ref, cells_ref, buf, *sums):
    half = slots // 2
    voxels = sums[0].shape[0] - 8
    f32 = jnp.float32

    def load(s, _):
        buf[pl.ds(pl.multiple_of(s * half, half), half), :] = got_ref[s, pl.ds(0, half), :].astype(f32)

    lax.fori_loop(0, devices, load, None)

    def clear(t, _):
        for each in sums:
            each[pl.ds(pl.multiple_of(t * TILE, TILE), TILE), :] = jnp.zeros((TILE, 128), f32)

    lax.fori_loop(0, voxels // TILE, clear, None)

    def source(s, _):
        here = count_ref[s]
        for h in range(2):
            some = jnp.clip(here - h * half, 0, half)

            def group(j, _):
                for u in range(GROUP):
                    r = j * GROUP + u
                    v = vox_ref[s * slots + h * half + r]
                    each = sums[2 * h + u % 2]
                    each[pl.ds(v, 1), :] += buf[pl.ds(s * half + r, 1), :]

            lax.fori_loop(0, (some + GROUP - 1) // GROUP, group, None)

    lax.fori_loop(0, devices, source, None)
    low = low_lanes(NZ)

    def finish(x, _):
        def parts(y):
            at = pl.ds(pl.multiple_of((x * CY + y) * NZ, NZ), NZ)
            return sums[0][at, :] + sums[1][at, :], sums[2][at, :] + sums[3][at, :]

        zero = jnp.zeros((NZ, 128), f32)
        for k in range(PAIRS):
            lo0, hi0 = parts(2 * k - 1) if k > 0 else (zero, zero)
            lo1, hi1 = parts(2 * k) if k < PAIRS - 1 else (zero, zero)
            tile = jnp.where(low, lo0, hi1) + swapped(jnp.where(low, lo1, hi0))
            cells_ref[x, k] = tile.astype(jnp.bfloat16)

    lax.fori_loop(0, cells_ref.shape[0], finish, None)


def inward_kernel(
    n_narrow, n_region, scale, first, second, collect, packed_table, center, grads, w,
    result, point_out, weight_out,
    table, block, back, buf, faces, left, right, top, bottom, corners, stack,
    products, kernels, parts, mine, rows_buf, out_buf,
    send, recv, halo_send, halo_recv, part_send, part_recv, all_send, all_recv,
):
    devices = n_narrow * n_region
    me = lax.axis_index("narrow") * n_region + lax.axis_index("region")
    half = buf.shape[0]
    f32, bf16 = jnp.float32, jnp.bfloat16
    low = low_lanes(NZ)
    rows_x = center.shape[0]
    meet_all(devices, n_region, me)
    moves = halo_moves(
        n_narrow, n_region, center, faces, left, right, top, bottom, corners, halo_send, halo_recv
    )
    start_halo(moves, center, faces)

    def widen(t, _):
        u = packed_table[pl.ds(pl.multiple_of(t * NZ, NZ), NZ), :]
        v = swapped(u)
        at = pl.multiple_of(t * 2 * NZ, 2 * NZ)
        table[pl.ds(at, NZ), :] = jnp.where(low, u, v)
        table[pl.ds(at + NZ, NZ), :] = jnp.where(low, v, u)

    lax.fori_loop(0, packed_table.shape[0] // NZ, widen, None)

    def fill(ref, at, other):
        paired_rows(first, second, table, other * half, half, buf)
        ref[at] = buf[...].astype(bf16)

    arrive = to_each(
        devices, n_region, me, lambda o: block.at[o], back.at[me], send, recv, lambda o: fill(block, o, o)
    )
    fill(back, me, me)
    stack_inside(stack, center)
    wait_halo(moves)
    stack_edges(stack, center, left, right, top, bottom, corners)

    span = (PAIRS - 1) * NZ

    def product(t, _):
        total = None
        for xp in range(rows_x // 2):
            here = grads[:, pl.ds(xp * span, span)]
            term = dot(here, window(stack, 2 * xp + t // 3, lax.rem(t, 3)))
            total = term if total is None else total + term
        products[t] = total

    lax.fori_loop(0, 12, product, None)

    kernels[...] = jnp.zeros_like(kernels)
    for pair in range(14):
        halves = []
        for e in range(2):
            t = 2 * pair + e
            if t >= 27:
                halves.append(jnp.zeros((64, 128), f32))
                continue
            a, b, d = t // 9, t // 3 % 3, t % 3
            value = None
            for p in range(2):
                q = b + p
                m, par = q // 2, q % 2
                some = None
                for i in range(2):
                    piece = products[(a + i) * 3 + d, pl.ds((2 * i + p) * 64, 64), pl.ds(m * 128, 128)]
                    some = piece if some is None else some + piece
                some = some if par == e else swapped(some)
                value = some if value is None else value + some
            halves.append(value)
        kernels[pl.ds(pair * 64, 64), :] = jnp.where(low, halves[0], halves[1])

    per = mine.shape[0]
    part = lambda o: kernels.at[pl.ds(pl.multiple_of(o * per, per), per)]
    parts_in = to_each(
        devices, n_region, me, part, parts.at[me], part_send, part_recv, lambda o: None
    )
    parts[me] = kernels[pl.ds(pl.multiple_of(me * per, per), per), :]

    def emit(xp, total):
        result[xp] = total.astype(bf16)

    convolve(stack, w, emit)

    parts_in()
    mine[...] = lax.fori_loop(
        1, devices, lambda s, total: total + parts[s], parts[0]
    ) * scale
    here = pl.ds(pl.multiple_of(me * per, per), per)
    gathered = to_each(
        devices, n_region, me, lambda o: mine, weight_out.at[here], all_send, all_recv, lambda o: None
    )
    weight_out[here, :] = mine[...]

    arrive()
    rows = devices * half

    def unpack(s, _):
        t = back[s].astype(f32)
        at = pl.multiple_of(s * half, half)
        rows_buf[pl.ds(at, half), :] = t
        rows_buf[pl.ds(rows + at, half), :] = swapped(t)

    lax.fori_loop(0, devices, unpack, None)
    few = out_buf.shape[0]
    points = point_out.shape[1]
    row_low = low_lanes(1)

    def gather(j, _):
        def group(g, _):
            for u in range(UNROLL):
                q = g * UNROLL + u
                a = rows_buf[pl.ds(collect[j * few + q], 1), :]
                b = rows_buf[pl.ds(collect[points // 2 + j * few + q], 1), :]
                out_buf[pl.ds(q, 1), :] = jnp.where(row_low, a, b)

        lax.fori_loop(0, few // UNROLL, group, None)
        t = out_buf[...].T.astype(bf16)
        at = pl.multiple_of(j * few, few)
        point_out[:, pl.ds(at, few)] = t[:64]
        point_out[:, pl.ds(points // 2 + at, few)] = t[64:]

    lax.fori_loop(0, points // 2 // few, gather, None)
    gathered()


def call(kernel, out_shape, kinds, out_kinds, scratch, collective_id, cost, *operands):
    where = {"s": pltpu.SMEM, "v": pltpu.VMEM, "a": pl.ANY}
    specs = [pl.BlockSpec(memory_space=where[k]) for k in out_kinds]
    remote = {} if collective_id is None else dict(collective_id=collective_id, has_side_effects=True)
    return pl.pallas_call(
        kernel,
        out_shape=out_shape,
        in_specs=[pl.BlockSpec(memory_space=where[k]) for k in kinds],
        out_specs=specs if len(specs) > 1 else specs[0],
        scratch_shapes=scratch,
        compiler_params=pltpu.CompilerParams(vmem_limit_bytes=56 << 20, **remote),
        cost_estimate=pl.CostEstimate(flops=0, bytes_accessed=cost, transcendentals=0),
    )(*operands)


def halo_scratch(rows_x):
    bf16 = jnp.bfloat16
    side = pltpu.VMEM((rows_x // 2, NZ, 128), bf16)
    end = pltpu.VMEM((PAIRS, NZ, 128), bf16)
    return [
        pltpu.VMEM((2, rows_x // 2, NZ, 128), bf16),
        side,
        side,
        end,
        end,
        pltpu.VMEM((4, NZ, 128), bf16),
        pltpu.VMEM((rows_x + 2, 3, PAIRS * NZ, 128), bf16),
    ]


def ranks(owner, devices):
    span = 128
    chunks = owner.shape[0] // span
    marks = owner.reshape(chunks, span)[:, :, None] == jnp.arange(devices, dtype=jnp.int32)
    ones = marks.astype(jnp.bfloat16)
    before = (jnp.arange(span)[:, None] > jnp.arange(span)[None, :]).astype(jnp.bfloat16)
    inner = jnp.einsum("ij,cjo->cio", before, ones, preferred_element_type=jnp.float32)
    tallies = jnp.sum(ones.astype(jnp.float32), axis=1)
    ahead = (jnp.arange(chunks)[:, None] > jnp.arange(chunks)[None, :]).astype(jnp.bfloat16)
    starts = jnp.einsum("ij,jo->io", ahead, tallies.astype(jnp.bfloat16), preferred_element_type=jnp.float32)
    slot = jnp.sum(jnp.where(marks, inner + starts[:, None, :], 0.0), axis=2)
    return slot.reshape(-1).astype(jnp.int32), jnp.sum(tallies, axis=0).astype(jnp.int32)


def block_weights(taps):
    ci, co = taps.shape[3:]
    shifted = [
        [jnp.pad(taps, ((i, 1 - i), (p, 1 - p), (0, 0), (0, 0), (0, 0))) for p in range(2)]
        for i in range(2)
    ]
    full = jnp.stack([jnp.stack(s) for s in shifted])
    return full.transpose(2, 4, 3, 5, 0, 1, 6).reshape(12, 4 * ci, 4 * co)


def shards(point_feats, point_owner, point_voxel, weight, cotangent):
    n_narrow = lax.axis_size("narrow")
    n_region = lax.axis_size("region")
    devices = n_narrow * n_region
    chans, points_here = point_feats.shape
    slots = 2 * points_here // devices
    half = slots // 2
    rows = devices * half
    rows_x = cotangent.shape[1]
    voxels = rows_x * CY * NZ
    f32, bf16, i32 = jnp.float32, jnp.bfloat16, jnp.int32
    spare = 16
    span = (PAIRS - 1) * NZ
    dma = pltpu.SemaphoreType.DMA

    w = weight.reshape(3, 3, chans, 3, chans)
    backward = block_weights(w[::-1, ::-1, :, ::-1, :].transpose(0, 1, 3, 2, 4))
    forward = block_weights(w.transpose(0, 1, 3, 4, 2))

    cot = cotangent.reshape(chans, rows_x, CY, NZ)
    grads = jnp.pad(cot, ((0, 0), (0, 0), (1, 1), (0, 0))).reshape(chans, rows_x, PAIRS, 2, NZ)
    grads = grads.transpose(1, 2, 4, 3, 0).reshape(rows_x, PAIRS, NZ, 2 * chans)
    flat = cotangent.reshape(chans, rows_x // 2, 2, CY // 2, 2, NZ)
    flat = flat.transpose(2, 4, 0, 1, 3, 5).reshape(4 * chans, voxels // 4)

    owner = point_owner[:, 0]
    slot, sent = ranks(owner, devices)
    marks = owner[:, None] == jnp.arange(devices, dtype=i32)
    index = jnp.arange(points_here, dtype=i32)
    values = jnp.stack([index // 64, index % 64, point_voxel // 128, point_voxel % 128], axis=1)
    named = jnp.where(marks[:, None, :], values[:, :, None], 0).astype(bf16).reshape(points_here, -1)
    seats = (slot[:, None] == jnp.arange(slots, dtype=i32)).astype(bf16)
    dealt = jnp.einsum("pa,ps->as", named, seats, preferred_element_type=f32)
    dealt = dealt.reshape(4, devices, slots)
    source = (dealt[0] * 64 + dealt[1]).astype(i32)
    filled = jnp.arange(slots, dtype=i32)[None, :] < sent[:, None]
    digits = jnp.concatenate(
        [
            jnp.where(filled, dealt[2], float(voxels // 128)),
            jnp.where(filled, dealt[3], float(voxels % 128)),
        ],
        axis=1,
    ).astype(bf16)
    digits = jnp.pad(digits, ((0, 0), (0, spare * 2 * chans - 2 * slots)))
    digits = digits.reshape(devices, spare, 2 * chans)
    feats = jnp.concatenate([point_feats, point_feats], axis=0).T.astype(f32)

    got, packed_table = call(
        functools.partial(outward_kernel, n_narrow, n_region),
        (
            jax.ShapeDtypeStruct((devices, half + spare, 2 * chans), bf16),
            jax.ShapeDtypeStruct((voxels // 2, 2 * chans), f32),
        ),
        "ssvvvv",
        "vv",
        [pltpu.VMEM((devices, half + spare, 2 * chans), bf16), pltpu.VMEM((half, 2 * chans), f32)]
        + halo_scratch(rows_x)
        + [dma((devices,)), dma((devices,)), dma((8,)), dma((8,))],
        0,
        60 << 20,
        source[:, :half].reshape(-1),
        source[:, half:].reshape(-1),
        feats,
        digits,
        grads,
        backward,
    )

    digits = got[:, half:].reshape(devices, spare * 2 * chans).astype(i32)
    got_vox = digits[:, :slots] * 128 + digits[:, slots : 2 * slots]
    count = jnp.sum((got_vox < voxels).astype(i32), axis=1)
    add_at = got_vox.reshape(-1)
    pick_at = jnp.where(got_vox < voxels, got_vox, 0)

    cells = call(
        functools.partial(splat_kernel, devices, slots),
        jax.ShapeDtypeStruct((rows_x, PAIRS, NZ, 2 * chans), bf16),
        "ssv",
        "v",
        [pltpu.VMEM((rows, 2 * chans), f32)] + [pltpu.VMEM((voxels + 8, 2 * chans), f32)] * 4,
        None,
        60 << 20,
        add_at,
        count,
        got,
    )

    seat = owner * half + slot % half
    side = slot // half
    wanted = index // (points_here // 2)
    collect = jnp.where(side == wanted, 0, rows) + seat
    total_cells = rows_x * n_region * CY * n_narrow * NZ
    kernel_rows = 1024
    per = kernel_rows // devices
    few = 128
    result, point_grad, kernels = call(
        functools.partial(inward_kernel, n_narrow, n_region, 1.0 / math.sqrt(total_cells)),
        (
            jax.ShapeDtypeStruct((rows_x // 2, span, 4 * chans), bf16),
            jax.ShapeDtypeStruct((chans, points_here), bf16),
            jax.ShapeDtypeStruct((kernel_rows, 2 * chans), f32),
        ),
        "sssvvvv",
        "vvv",
        [
            pltpu.VMEM((voxels, 2 * chans), f32),
            pltpu.VMEM((devices, half, 2 * chans), bf16),
            pltpu.VMEM((devices, half, 2 * chans), bf16),
            pltpu.VMEM((half, 2 * chans), f32),
        ]
        + halo_scratch(rows_x)
        + [
            pltpu.VMEM((12, 4 * chans, 4 * chans), f32),
            pltpu.VMEM((kernel_rows, 2 * chans), f32),
            pltpu.VMEM((devices, per, 2 * chans), f32),
            pltpu.VMEM((per, 2 * chans), f32),
            pltpu.VMEM((2 * rows, 2 * chans), f32),
            pltpu.VMEM((few, 2 * chans), f32),
        ]
        + [dma((devices,)), dma((devices,)), dma((8,)), dma((8,))]
        + [dma((devices,))] * 4,
        1,
        100 << 20,
        pick_at[:, :half].reshape(-1),
        pick_at[:, half:].reshape(-1),
        collect,
        packed_table,
        cells,
        flat,
        forward,
    )
    conv_out = result.reshape(rows_x // 2, CY // 2, NZ, 2, 2, chans).transpose(5, 0, 3, 1, 4, 2)
    conv_out = conv_out.reshape(chans, rows_x, CY * NZ)
    kernels = kernels.reshape(kernel_rows // 64, 64, 2, 64).transpose(0, 2, 1, 3).reshape(-1, 64, 64)
    weight_grad = kernels[:27].reshape(9, 3, 64, 64).transpose(0, 2, 1, 3).reshape(9, 64, 192)
    return (conv_out, point_grad, weight_grad)


def solution(mesh):
    in_specs = (
        P(None, AXES),
        P(AXES, None),
        P(AXES),
        P(),
        P(None, "region", "narrow"),
    )
    out_specs = (P(None, "region", "narrow"), P(None, AXES), P())
    return jax.shard_map(shards, mesh=mesh, in_specs=in_specs, out_specs=out_specs, check_vma=False)
```

```python
import functools
import math

import jax
import jax.numpy as jnp
from jax import lax
from jax.experimental import pallas as pl
from jax.experimental.pallas import tpu as pltpu
from jax.sharding import PartitionSpec as P

NZ = 64
CY = 8
AXES = ("narrow", "region")
GROUP = 8
UNROLL = 16
TILE = 512
PAIRS = CY // 2 + 1
MESH = pl.DeviceIdType.MESH


def dot(a, b):
    return jnp.dot(a, b, preferred_element_type=jnp.float32)


def low_lanes(rows):
    return lax.broadcasted_iota(jnp.int32, (rows, 128), 1) < 64


def swapped(t):
    return pltpu.roll(t, 64, 1)


def device(flat, n_region):
    return (flat // n_region, lax.rem(flat, n_region))


def greet_all(devices, n_region, me):
    barrier = pltpu.get_barrier_semaphore()

    def greet(s, _):
        other = device(lax.rem(me + s, devices), n_region)
        pl.semaphore_signal(barrier, inc=1, device_id=other, device_id_type=MESH)

    lax.fori_loop(1, devices, greet, None)
    return lambda: pl.semaphore_wait(barrier, devices - 1)


def halo_moves(n_narrow, n_region, center, faces, left, right, top, bottom, corners, send, recv):
    n, r = lax.axis_index("narrow"), lax.axis_index("region")
    last = center.shape[0] - 1
    west, east = lax.rem(n + n_narrow - 1, n_narrow), lax.rem(n + 1, n_narrow)
    north, south = lax.rem(r + n_region - 1, n_region), lax.rem(r + 1, n_region)
    w, e, u, d = n > 0, n < n_narrow - 1, r > 0, r < n_region - 1
    both = jnp.logical_and
    table = [
        (w, e, (west, r), faces.at[0], right),
        (e, w, (east, r), faces.at[1], left),
        (u, d, (n, north), center.at[0], bottom),
        (d, u, (n, south), center.at[last], top),
        (both(w, u), both(e, d), (west, north), center.at[0, 0], corners.at[3]),
        (both(e, u), both(w, d), (east, north), center.at[0, PAIRS - 1], corners.at[2]),
        (both(w, d), both(e, u), (west, south), center.at[last, 0], corners.at[1]),
        (both(e, d), both(w, u), (east, south), center.at[last, PAIRS - 1], corners.at[0]),
    ]
    return [
        (
            sends,
            gets,
            pltpu.make_async_remote_copy(
                src_ref=source,
                dst_ref=target,
                send_sem=send.at[i],
                recv_sem=recv.at[i],
                device_id=where,
                device_id_type=MESH,
            ),
            target,
        )
        for i, (sends, gets, where, source, target) in enumerate(table)
    ]


def start_halo(moves, center, faces):
    half_x = center.shape[0] // 2
    f32 = jnp.float32

    def face(x, _):
        for i, k in ((0, 0), (1, PAIRS - 1)):
            tile = center[x, k].astype(f32) + swapped(center[x + half_x, k].astype(f32))
            faces[i, x] = tile.astype(jnp.bfloat16)

    lax.fori_loop(0, half_x, face, None)
    for sends, gets, copy, target in moves:

        @pl.when(sends)
        def _():
            copy.start()

        @pl.when(jnp.logical_not(gets))
        def _():
            target[...] = jnp.zeros(target.shape, target.dtype)


def wait_halo(moves):
    for sends, gets, copy, _ in moves:

        @pl.when(gets)
        def _():
            copy.wait_recv()

        @pl.when(sends)
        def _():
            copy.wait_send()


def put(stack, x, k, t):
    row = lax.broadcasted_iota(jnp.int32, t.shape, 0)
    at = pl.ds(k * NZ, NZ)
    up = jnp.where(row == 0, 0.0, pltpu.roll(t, 1, 0))
    down = jnp.where(row == NZ - 1, 0.0, pltpu.roll(t, NZ - 1, 0))
    stack[x, 0, at, :] = up.astype(jnp.bfloat16)
    stack[x, 1, at, :] = t.astype(jnp.bfloat16)
    stack[x, 2, at, :] = down.astype(jnp.bfloat16)


def stack_inside(stack, center):
    def plane(x, _):
        for k in range(1, PAIRS - 1):
            put(stack, x + 1, k, center[x, k].astype(jnp.float32))

    lax.fori_loop(0, center.shape[0], plane, None)


def stack_edges(stack, center, left, right, top, bottom, corners):
    rows_x = center.shape[0]
    half_x = rows_x // 2
    f32 = jnp.float32
    low = low_lanes(NZ)
    end = PAIRS - 1

    def sides(x, _):
        from_left, from_right = left[x].astype(f32), right[x].astype(f32)
        for at, l, r in (
            (x, from_left, from_right),
            (x + half_x, swapped(from_left), swapped(from_right)),
        ):
            put(stack, at + 1, 0, center[at, 0].astype(f32) + jnp.where(low, l, 0.0))
            put(stack, at + 1, end, center[at, end].astype(f32) + jnp.where(low, 0.0, r))

    lax.fori_loop(0, half_x, sides, None)
    for x, rows, c in ((0, top, 0), (rows_x + 1, bottom, 2)):
        for k in range(PAIRS):
            t = rows[k].astype(f32)
            if k == 0:
                t += corners[c].astype(f32)
            if k == end:
                t += corners[c + 1].astype(f32)
            put(stack, x, k, t)


def window(stack, x, d):
    rows = (PAIRS - 1) * NZ
    return jnp.concatenate([stack[x, d, pl.ds(0, rows), :], stack[x, d, pl.ds(NZ, rows), :]], axis=1)


def spread_weights(w, block):
    zero = jnp.zeros((64, 64), jnp.float32)
    for a in (0, 4):
        w[a] = jnp.zeros(w.shape[1:], w.dtype)
    for a in range(3):
        for d in range(3):
            for q in range(4):
                left = block(a, q, d) if q < 3 else zero
                right = block(a, q - 1, d) if q > 0 else zero
                both = jnp.concatenate([left, right], axis=1)
                w[a + 1, d, pl.ds(q * 64, 64), :] = both.astype(jnp.bfloat16)


def convolve(stack, w, emit):
    def step(xp, _):
        total = None
        for i in range(4):
            for d in range(3):
                both = jnp.concatenate([w[i + 1, d], w[i, d]], axis=1)
                term = dot(window(stack, 2 * xp + i, d), both)
                total = term if total is None else total + term
        emit(xp, total)

    lax.fori_loop(0, (stack.shape[0] - 2) // 2, step, None)


def to_each(devices, n_region, me, source, target, send, recv, visit):
    def copy(s):
        other = lax.rem(me + s, devices)
        return pltpu.make_async_remote_copy(
            src_ref=source(other),
            dst_ref=target,
            send_sem=send.at[s],
            recv_sem=recv.at[s],
            device_id=device(other, n_region),
            device_id_type=MESH,
        )

    def go(s, _):
        visit(lax.rem(me + s, devices))
        copy(s).start()

    def finish(s, _):
        copy(s).wait_recv()
        copy(s).wait_send()

    lax.fori_loop(1, devices, go, None)
    return lambda: lax.fori_loop(1, devices, finish, None)


def paired_rows(first, second, table, base, rows, buf):
    low = low_lanes(1)

    def group(j, _):
        for u in range(UNROLL):
            q = j * UNROLL + u
            a = table[pl.ds(first[base + q], 1), :]
            b = table[pl.ds(second[base + q], 1), :]
            buf[pl.ds(q, 1), :] = jnp.where(low, a, b)

    lax.fori_loop(0, rows // UNROLL, group, None)


def outward_kernel(
    n_narrow, n_region, first, second, feats, digits, grads, weight,
    got, table,
    center, w, block, buf, faces, left, right, top, bottom, corners, stack,
    send, recv, halo_send, halo_recv,
):
    devices = n_narrow * n_region
    me = lax.axis_index("narrow") * n_region + lax.axis_index("region")
    half = buf.shape[0]
    spare = digits.shape[1]
    f32 = jnp.float32
    met = greet_all(devices, n_region, me)
    zero = jnp.zeros((NZ, 64), f32)

    def pairs(x, _):
        for k in range(PAIRS):
            a = grads[x, 2 * k - 1].astype(f32) if k > 0 else zero
            b = grads[x, 2 * k].astype(f32) if k < PAIRS - 1 else zero
            center[x, k] = jnp.concatenate([a, b], axis=1).astype(jnp.bfloat16)

    lax.fori_loop(0, center.shape[0], pairs, None)
    met()
    moves = halo_moves(
        n_narrow, n_region, center, faces, left, right, top, bottom, corners, halo_send, halo_recv
    )
    start_halo(moves, center, faces)

    def fill(ref, at, other):
        paired_rows(first, second, feats, other * half, half, buf)
        ref[at, pl.ds(0, half), :] = buf[...].astype(jnp.bfloat16)
        ref[at, pl.ds(half, spare), :] = digits[other]

    arrive = to_each(
        devices, n_region, me, lambda o: block.at[o], got.at[me], send, recv, lambda o: fill(block, o, o)
    )
    fill(got, me, me)
    stack_inside(stack, center)
    wait_halo(moves)
    stack_edges(stack, center, left, right, top, bottom, corners)
    rows = (PAIRS - 1) * NZ
    spread_weights(
        w, lambda a, b, d: weight[8 - 3 * a - b, :, pl.ds(0, 192)].astype(f32)[:, 128 - d * 64 : 192 - d * 64]
    )

    def emit(xp, total):
        for i in range(2):
            at = pl.multiple_of((2 * xp + i) * rows, rows)
            table[pl.ds(at, rows), :] = total[:, i * 128 : (i + 1) * 128]

    convolve(stack, w, emit)
    arrive()


def splat_kernel(devices, slots, vox_ref, count_ref, got_ref, cells_ref, buf, *sums):
    half = slots // 2
    voxels = sums[0].shape[0] - 8
    f32 = jnp.float32

    def load(s, _):
        buf[pl.ds(pl.multiple_of(s * half, half), half), :] = got_ref[s, pl.ds(0, half), :].astype(f32)

    lax.fori_loop(0, devices, load, None)

    def clear(t, _):
        for each in sums:
            each[pl.ds(pl.multiple_of(t * TILE, TILE), TILE), :] = jnp.zeros((TILE, 128), f32)

    lax.fori_loop(0, voxels // TILE, clear, None)

    def source(s, _):
        here = count_ref[s]
        for h in range(2):
            some = jnp.clip(here - h * half, 0, half)

            def group(j, _):
                for u in range(GROUP):
                    r = j * GROUP + u
                    v = vox_ref[s * slots + h * half + r]
                    each = sums[2 * h + u % 2]
                    each[pl.ds(v, 1), :] += buf[pl.ds(s * half + r, 1), :]

            lax.fori_loop(0, (some + GROUP - 1) // GROUP, group, None)

    lax.fori_loop(0, devices, source, None)
    low = low_lanes(NZ)

    def finish(x, _):
        def parts(y):
            at = pl.ds(pl.multiple_of((x * CY + y) * NZ, NZ), NZ)
            return sums[0][at, :] + sums[1][at, :], sums[2][at, :] + sums[3][at, :]

        zero = jnp.zeros((NZ, 128), f32)
        for k in range(PAIRS):
            lo0, hi0 = parts(2 * k - 1) if k > 0 else (zero, zero)
            lo1, hi1 = parts(2 * k) if k < PAIRS - 1 else (zero, zero)
            tile = jnp.where(low, lo0, hi1) + swapped(jnp.where(low, lo1, hi0))
            cells_ref[x, k] = tile.astype(jnp.bfloat16)

    lax.fori_loop(0, cells_ref.shape[0], finish, None)


def inward_kernel(
    n_narrow, n_region, scale, first, second, collect, packed_table, center, cot, weight,
    result, point_out, weight_out,
    w, grads, planes, table, block, back, buf, faces, left, right, top, bottom, corners, stack,
    products, kernels, parts, mine, rows_buf, out_buf,
    send, recv, halo_send, halo_recv, part_send, part_recv, all_send, all_recv,
):
    devices = n_narrow * n_region
    me = lax.axis_index("narrow") * n_region + lax.axis_index("region")
    half = buf.shape[0]
    f32, bf16 = jnp.float32, jnp.bfloat16
    low = low_lanes(NZ)
    rows_x = center.shape[0]
    met = greet_all(devices, n_region, me)
    spread_weights(w, lambda a, b, d: weight[3 * a + b, pl.ds(d * 64, 64), :].astype(f32))
    met()
    moves = halo_moves(
        n_narrow, n_region, center, faces, left, right, top, bottom, corners, halo_send, halo_recv
    )
    start_halo(moves, center, faces)

    def widen(t, _):
        u = packed_table[pl.ds(pl.multiple_of(t * NZ, NZ), NZ), :]
        v = swapped(u)
        at = pl.multiple_of(t * 2 * NZ, 2 * NZ)
        table[pl.ds(at, NZ), :] = jnp.where(low, u, v)
        table[pl.ds(at + NZ, NZ), :] = jnp.where(low, v, u)

    lax.fori_loop(0, packed_table.shape[0] // NZ, widen, None)

    def fill(ref, at, other):
        paired_rows(first, second, table, other * half, half, buf)
        ref[at] = buf[...].astype(bf16)

    arrive = to_each(
        devices, n_region, me, lambda o: block.at[o], back.at[me], send, recv, lambda o: fill(block, o, o)
    )
    fill(back, me, me)
    stack_inside(stack, center)
    wait_halo(moves)
    stack_edges(stack, center, left, right, top, bottom, corners)

    span = (PAIRS - 1) * NZ
    outs = cot.shape[0]

    def lay(o, _):
        for j in range(CY // 2):
            t = cot[o, :, pl.ds(j * 128, 128)].astype(f32)
            planes[j, pl.ds(pl.multiple_of(o * rows_x, 8), rows_x), :] = t

    lax.fori_loop(0, outs, lay, None)

    def turn(xp, _):
        for i in range(2):
            some = pl.ds(2 * xp + i, outs, stride=rows_x)
            for m in range(2):
                a, b = planes[2 * m, some, :], planes[2 * m + 1, some, :]
                at = pl.ds(pl.multiple_of(xp * span + m * 128, 128), 128)
                grads[pl.ds(2 * i * 64, 64), at] = jnp.where(low, a, swapped(b)).astype(bf16)
                grads[pl.ds((2 * i + 1) * 64, 64), at] = jnp.where(low, swapped(a), b).astype(bf16)

    lax.fori_loop(0, rows_x // 2, turn, None)

    def product(t, _):
        total = None
        for xp in range(rows_x // 2):
            here = grads[:, pl.ds(xp * span, span)]
            term = dot(here, window(stack, 2 * xp + t // 3, lax.rem(t, 3)))
            total = term if total is None else total + term
        products[t] = total

    lax.fori_loop(0, 12, product, None)

    kernels[...] = jnp.zeros_like(kernels)
    for pair in range(14):
        halves = []
        for e in range(2):
            t = 2 * pair + e
            if t >= 27:
                halves.append(jnp.zeros((64, 128), f32))
                continue
            a, b, d = t // 9, t // 3 % 3, t % 3
            value = None
            for p in range(2):
                q = b + p
                m, par = q // 2, q % 2
                some = None
                for i in range(2):
                    piece = products[(a + i) * 3 + d, pl.ds((2 * i + p) * 64, 64), pl.ds(m * 128, 128)]
                    some = piece if some is None else some + piece
                some = some if par == e else swapped(some)
                value = some if value is None else value + some
            halves.append(value)
        kernels[pl.ds(pair * 64, 64), :] = jnp.where(low, halves[0], halves[1])

    per = mine.shape[0]
    part = lambda o: kernels.at[pl.ds(pl.multiple_of(o * per, per), per)]
    parts_in = to_each(
        devices, n_region, me, part, parts.at[me], part_send, part_recv, lambda o: None
    )
    parts[me] = kernels[pl.ds(pl.multiple_of(me * per, per), per), :]

    def emit(xp, total):
        t = total.T
        for i in range(2):
            at = pl.ds(pl.multiple_of((2 * xp + i) * 64, 64), 64)
            for m in range(2):
                a = t[i * 128 : i * 128 + 64, m * 128 : (m + 1) * 128]
                b = t[i * 128 + 64 : i * 128 + 128, m * 128 : (m + 1) * 128]
                planes[2 * m, at, :] = jnp.where(low, a, swapped(b))
                planes[2 * m + 1, at, :] = jnp.where(low, swapped(a), b)

    convolve(stack, w, emit)

    def settle(o, _):
        for j in range(CY // 2):
            t = planes[j, pl.ds(o, rows_x, stride=outs), :]
            result[o, :, pl.ds(j * 128, 128)] = t.astype(bf16)

    lax.fori_loop(0, outs, settle, None)

    parts_in()
    mine[...] = lax.fori_loop(
        1, devices, lambda s, total: total + parts[s], parts[0]
    ) * scale
    here = pl.ds(pl.multiple_of(me * per, per), per)
    gathered = to_each(
        devices, n_region, me, lambda o: mine, weight_out.at[here], all_send, all_recv, lambda o: None
    )
    weight_out[here, :] = mine[...]

    arrive()
    rows = devices * half

    def unpack(s, _):
        t = back[s].astype(f32)
        at = pl.multiple_of(s * half, half)
        rows_buf[pl.ds(at, half), :] = t
        rows_buf[pl.ds(rows + at, half), :] = swapped(t)

    lax.fori_loop(0, devices, unpack, None)
    few = out_buf.shape[0]
    points = point_out.shape[1]
    row_low = low_lanes(1)

    def gather(j, _):
        def group(g, _):
            for u in range(UNROLL):
                q = g * UNROLL + u
                a = rows_buf[pl.ds(collect[j * few + q], 1), :]
                b = rows_buf[pl.ds(collect[points // 2 + j * few + q], 1), :]
                out_buf[pl.ds(q, 1), :] = jnp.where(row_low, a, b)

        lax.fori_loop(0, few // UNROLL, group, None)
        t = out_buf[...].T.astype(bf16)
        at = pl.multiple_of(j * few, few)
        point_out[:, pl.ds(at, few)] = t[:64]
        point_out[:, pl.ds(points // 2 + at, few)] = t[64:]

    lax.fori_loop(0, points // 2 // few, gather, None)
    gathered()


def call(kernel, out_shape, kinds, out_kinds, scratch, collective_id, cost, *operands):
    where = {"s": pltpu.SMEM, "v": pltpu.VMEM, "a": pl.ANY}
    specs = [pl.BlockSpec(memory_space=where[k]) for k in out_kinds]
    remote = {} if collective_id is None else dict(collective_id=collective_id, has_side_effects=True)
    return pl.pallas_call(
        kernel,
        out_shape=out_shape,
        in_specs=[pl.BlockSpec(memory_space=where[k]) for k in kinds],
        out_specs=specs if len(specs) > 1 else specs[0],
        scratch_shapes=scratch,
        compiler_params=pltpu.CompilerParams(vmem_limit_bytes=56 << 20, **remote),
        cost_estimate=pl.CostEstimate(flops=0, bytes_accessed=cost, transcendentals=0),
    )(*operands)


def halo_scratch(rows_x):
    bf16 = jnp.bfloat16
    side = pltpu.VMEM((rows_x // 2, NZ, 128), bf16)
    end = pltpu.VMEM((PAIRS, NZ, 128), bf16)
    return [
        pltpu.VMEM((2, rows_x // 2, NZ, 128), bf16),
        side,
        side,
        end,
        end,
        pltpu.VMEM((4, NZ, 128), bf16),
        pltpu.VMEM((rows_x + 2, 3, PAIRS * NZ, 128), bf16),
    ]


def ranks(owner, devices):
    span = 128
    chunks = owner.shape[0] // span
    marks = owner.reshape(chunks, span)[:, :, None] == jnp.arange(devices, dtype=jnp.int32)
    ones = marks.astype(jnp.bfloat16)
    before = (jnp.arange(span)[:, None] > jnp.arange(span)[None, :]).astype(jnp.bfloat16)
    inner = jnp.einsum("ij,cjo->cio", before, ones, preferred_element_type=jnp.float32)
    tallies = jnp.sum(ones.astype(jnp.float32), axis=1)
    ahead = (jnp.arange(chunks)[:, None] > jnp.arange(chunks)[None, :]).astype(jnp.bfloat16)
    starts = jnp.einsum("ij,jo->io", ahead, tallies.astype(jnp.bfloat16), preferred_element_type=jnp.float32)
    slot = jnp.sum(jnp.where(marks, inner + starts[:, None, :], 0.0), axis=2)
    return slot.reshape(-1).astype(jnp.int32), jnp.sum(tallies, axis=0).astype(jnp.int32)


def shards(point_feats, point_owner, point_voxel, weight, cotangent):
    n_narrow = lax.axis_size("narrow")
    n_region = lax.axis_size("region")
    devices = n_narrow * n_region
    chans, points_here = point_feats.shape
    slots = 2 * points_here // devices
    half = slots // 2
    rows = devices * half
    rows_x = cotangent.shape[1]
    voxels = rows_x * CY * NZ
    f32, bf16, i32 = jnp.float32, jnp.bfloat16, jnp.int32
    spare = 16
    dma = pltpu.SemaphoreType.DMA

    grads = cotangent.reshape(chans, rows_x, CY, NZ).transpose(1, 2, 3, 0)
    weights = pltpu.VMEM((5, 3, 4 * chans, 2 * chans), bf16)

    owner = point_owner[:, 0]
    slot, sent = ranks(owner, devices)
    marks = owner[:, None] == jnp.arange(devices, dtype=i32)
    index = jnp.arange(points_here, dtype=i32)
    values = jnp.stack([index // 64, index % 64, point_voxel // 128, point_voxel % 128], axis=1)
    named = jnp.where(marks[:, None, :], values[:, :, None], 0).astype(bf16).reshape(points_here, -1)
    seats = (slot[:, None] == jnp.arange(slots, dtype=i32)).astype(bf16)
    dealt = jnp.einsum("pa,ps->as", named, seats, preferred_element_type=f32)
    dealt = dealt.reshape(4, devices, slots)
    source = (dealt[0] * 64 + dealt[1]).astype(i32)
    filled = jnp.arange(slots, dtype=i32)[None, :] < sent[:, None]
    digits = jnp.concatenate(
        [
            jnp.where(filled, dealt[2], float(voxels // 128)),
            jnp.where(filled, dealt[3], float(voxels % 128)),
        ],
        axis=1,
    ).astype(bf16)
    digits = jnp.pad(digits, ((0, 0), (0, spare * 2 * chans - 2 * slots)))
    digits = digits.reshape(devices, spare, 2 * chans)
    feats = jnp.concatenate([point_feats, point_feats], axis=0).T.astype(f32)

    got, packed_table = call(
        functools.partial(outward_kernel, n_narrow, n_region),
        (
            jax.ShapeDtypeStruct((devices, half + spare, 2 * chans), bf16),
            jax.ShapeDtypeStruct((voxels // 2, 2 * chans), f32),
        ),
        "ssvvvv",
        "vv",
        [
            pltpu.VMEM((rows_x, PAIRS, NZ, 2 * chans), bf16),
            weights,
            pltpu.VMEM((devices, half + spare, 2 * chans), bf16),
            pltpu.VMEM((half, 2 * chans), f32),
        ]
        + halo_scratch(rows_x)
        + [dma((devices,)), dma((devices,)), dma((8,)), dma((8,))],
        0,
        60 << 20,
        source[:, :half].reshape(-1),
        source[:, half:].reshape(-1),
        feats,
        digits,
        grads,
        weight,
    )

    digits = got[:, half:].reshape(devices, spare * 2 * chans).astype(i32)
    got_vox = digits[:, :slots] * 128 + digits[:, slots : 2 * slots]
    count = jnp.sum((got_vox < voxels).astype(i32), axis=1)
    add_at = got_vox.reshape(-1)
    pick_at = jnp.where(got_vox < voxels, got_vox, 0)

    cells = call(
        functools.partial(splat_kernel, devices, slots),
        jax.ShapeDtypeStruct((rows_x, PAIRS, NZ, 2 * chans), bf16),
        "ssv",
        "v",
        [pltpu.VMEM((rows, 2 * chans), f32)] + [pltpu.VMEM((voxels + 8, 2 * chans), f32)] * 4,
        None,
        60 << 20,
        add_at,
        count,
        got,
    )

    seat = owner * half + slot % half
    side = slot // half
    wanted = index // (points_here // 2)
    collect = jnp.where(side == wanted, 0, rows) + seat
    total_cells = rows_x * n_region * CY * n_narrow * NZ
    kernel_rows = 1024
    per = kernel_rows // devices
    few = 128
    result, point_grad, kernels = call(
        functools.partial(inward_kernel, n_narrow, n_region, 1.0 / math.sqrt(total_cells)),
        (
            jax.ShapeDtypeStruct((chans, rows_x, CY * NZ), bf16),
            jax.ShapeDtypeStruct((chans, points_here), bf16),
            jax.ShapeDtypeStruct((kernel_rows, 2 * chans), f32),
        ),
        "sssvvvv",
        "vvv",
        [
            weights,
            pltpu.VMEM((4 * chans, voxels // 4), bf16),
            pltpu.VMEM((CY // 2, rows_x * chans, 2 * NZ), f32),
            pltpu.VMEM((voxels, 2 * chans), f32),
            pltpu.VMEM((devices, half, 2 * chans), bf16),
            pltpu.VMEM((devices, half, 2 * chans), bf16),
            pltpu.VMEM((half, 2 * chans), f32),
        ]
        + halo_scratch(rows_x)
        + [
            pltpu.VMEM((12, 4 * chans, 4 * chans), f32),
            pltpu.VMEM((kernel_rows, 2 * chans), f32),
            pltpu.VMEM((devices, per, 2 * chans), f32),
            pltpu.VMEM((per, 2 * chans), f32),
            pltpu.VMEM((2 * rows, 2 * chans), f32),
            pltpu.VMEM((few, 2 * chans), f32),
        ]
        + [dma((devices,)), dma((devices,)), dma((8,)), dma((8,))]
        + [dma((devices,))] * 4,
        1,
        100 << 20,
        pick_at[:, :half].reshape(-1),
        pick_at[:, half:].reshape(-1),
        collect,
        packed_table,
        cells,
        cotangent,
        weight.transpose(0, 2, 1),
    )
    kernels = kernels.reshape(kernel_rows // 64, 64, 2, 64).transpose(0, 2, 1, 3).reshape(-1, 64, 64)
    weight_grad = kernels[:27].reshape(9, 3, 64, 64).transpose(0, 2, 1, 3).reshape(9, 64, 192)
    return (result, point_grad, weight_grad)


def solution(mesh):
    in_specs = (
        P(None, AXES),
        P(AXES, None),
        P(AXES),
        P(),
        P(None, "region", "narrow"),
    )
    out_specs = (P(None, "region", "narrow"), P(None, AXES), P())
    return jax.shard_map(shards, mesh=mesh, in_specs=in_specs, out_specs=out_specs, check_vma=False)
```

```python
import functools
import math

import jax
import jax.numpy as jnp
from jax import lax
from jax.experimental import pallas as pl
from jax.experimental.pallas import tpu as pltpu
from jax.sharding import PartitionSpec as P

NZ = 64
CY = 8
AXES = ("narrow", "region")
UNROLL = 16
COPIES = 4
VISITS = 128
PAIRS = CY // 2 + 1
MESH = pl.DeviceIdType.MESH


def dot(a, b):
    return jnp.dot(a, b, preferred_element_type=jnp.float32)


def low_lanes(rows):
    return lax.broadcasted_iota(jnp.int32, (rows, 128), 1) < 64


def swapped(t):
    return pltpu.roll(t, 64, 1)


def device(flat, n_region):
    return (flat // n_region, lax.rem(flat, n_region))


def greet_all(devices, n_region, me):
    barrier = pltpu.get_barrier_semaphore()

    def greet(s, _):
        other = device(lax.rem(me + s, devices), n_region)
        pl.semaphore_signal(barrier, inc=1, device_id=other, device_id_type=MESH)

    lax.fori_loop(1, devices, greet, None)
    return lambda: pl.semaphore_wait(barrier, devices - 1)


def halo_moves(n_narrow, n_region, center, faces, left, right, top, bottom, corners, send, recv):
    n, r = lax.axis_index("narrow"), lax.axis_index("region")
    last = center.shape[0] - 1
    west, east = lax.rem(n + n_narrow - 1, n_narrow), lax.rem(n + 1, n_narrow)
    north, south = lax.rem(r + n_region - 1, n_region), lax.rem(r + 1, n_region)
    w, e, u, d = n > 0, n < n_narrow - 1, r > 0, r < n_region - 1
    both = jnp.logical_and
    table = [
        (w, e, (west, r), faces.at[0], right),
        (e, w, (east, r), faces.at[1], left),
        (u, d, (n, north), center.at[0], bottom),
        (d, u, (n, south), center.at[last], top),
        (both(w, u), both(e, d), (west, north), center.at[0, 0], corners.at[3]),
        (both(e, u), both(w, d), (east, north), center.at[0, PAIRS - 1], corners.at[2]),
        (both(w, d), both(e, u), (west, south), center.at[last, 0], corners.at[1]),
        (both(e, d), both(w, u), (east, south), center.at[last, PAIRS - 1], corners.at[0]),
    ]
    return [
        (
            sends,
            gets,
            pltpu.make_async_remote_copy(
                src_ref=source,
                dst_ref=target,
                send_sem=send.at[i],
                recv_sem=recv.at[i],
                device_id=where,
                device_id_type=MESH,
            ),
            target,
        )
        for i, (sends, gets, where, source, target) in enumerate(table)
    ]


def start_halo(moves, center, faces):
    half_x = center.shape[0] // 2
    f32 = jnp.float32

    def face(x, _):
        for i, k in ((0, 0), (1, PAIRS - 1)):
            tile = center[x, k].astype(f32) + swapped(center[x + half_x, k].astype(f32))
            faces[i, x] = tile.astype(jnp.bfloat16)

    lax.fori_loop(0, half_x, face, None)
    for sends, gets, copy, target in moves:

        @pl.when(sends)
        def _():
            copy.start()

        @pl.when(jnp.logical_not(gets))
        def _():
            target[...] = jnp.zeros(target.shape, target.dtype)


def wait_halo(moves):
    for sends, gets, copy, _ in moves:

        @pl.when(gets)
        def _():
            copy.wait_recv()

        @pl.when(sends)
        def _():
            copy.wait_send()


def put(stack, x, k, t):
    row = lax.broadcasted_iota(jnp.int32, t.shape, 0)
    at = pl.ds(k * NZ, NZ)
    up = jnp.where(row == 0, 0.0, pltpu.roll(t, 1, 0))
    down = jnp.where(row == NZ - 1, 0.0, pltpu.roll(t, NZ - 1, 0))
    stack[x, 0, at, :] = up.astype(jnp.bfloat16)
    stack[x, 1, at, :] = t.astype(jnp.bfloat16)
    stack[x, 2, at, :] = down.astype(jnp.bfloat16)


def stack_inside(stack, center):
    def plane(x, _):
        for k in range(1, PAIRS - 1):
            put(stack, x + 1, k, center[x, k].astype(jnp.float32))

    lax.fori_loop(0, center.shape[0], plane, None)


def stack_edges(stack, center, left, right, top, bottom, corners):
    rows_x = center.shape[0]
    half_x = rows_x // 2
    f32 = jnp.float32
    low = low_lanes(NZ)
    end = PAIRS - 1

    def sides(x, _):
        from_left, from_right = left[x].astype(f32), right[x].astype(f32)
        for at, l, r in (
            (x, from_left, from_right),
            (x + half_x, swapped(from_left), swapped(from_right)),
        ):
            put(stack, at + 1, 0, center[at, 0].astype(f32) + jnp.where(low, l, 0.0))
            put(stack, at + 1, end, center[at, end].astype(f32) + jnp.where(low, 0.0, r))

    lax.fori_loop(0, half_x, sides, None)
    for x, rows, c in ((0, top, 0), (rows_x + 1, bottom, 2)):
        for k in range(PAIRS):
            t = rows[k].astype(f32)
            if k == 0:
                t += corners[c].astype(f32)
            if k == end:
                t += corners[c + 1].astype(f32)
            put(stack, x, k, t)


def window(stack, x, d):
    rows = (PAIRS - 1) * NZ
    return jnp.concatenate([stack[x, d, pl.ds(0, rows), :], stack[x, d, pl.ds(NZ, rows), :]], axis=1)


def spread_weights(w, block):
    zero = jnp.zeros((64, 64), jnp.float32)
    for a in (0, 4):
        w[a] = jnp.zeros(w.shape[1:], w.dtype)
    for a in range(3):
        for d in range(3):
            for q in range(4):
                left = block(a, q, d) if q < 3 else zero
                right = block(a, q - 1, d) if q > 0 else zero
                both = jnp.concatenate([left, right], axis=1)
                w[a + 1, d, pl.ds(q * 64, 64), :] = both.astype(jnp.bfloat16)


def convolve(stack, w, emit):
    def step(xp, _):
        total = None
        for i in range(4):
            for d in range(3):
                both = jnp.concatenate([w[i + 1, d], w[i, d]], axis=1)
                term = dot(window(stack, 2 * xp + i, d), both)
                total = term if total is None else total + term
        emit(xp, total)

    lax.fori_loop(0, (stack.shape[0] - 2) // 2, step, None)


def to_each(devices, n_region, me, source, target, send, recv, visit=None):
    def copy(s):
        other = lax.rem(me + s, devices)
        return pltpu.make_async_remote_copy(
            src_ref=source(other),
            dst_ref=target,
            send_sem=send.at[s],
            recv_sem=recv.at[s],
            device_id=device(other, n_region),
            device_id_type=MESH,
        )

    def go(s, _):
        if visit is not None:
            visit(lax.rem(me + s, devices))
        copy(s).start()

    def finish(s, _):
        copy(s).wait_recv()
        copy(s).wait_send()

    lax.fori_loop(1, devices, go, None)
    return lambda: lax.fori_loop(1, devices, finish, None)


def paired_rows(first, second, table, base, rows, buf):
    low = low_lanes(1)

    def group(j, _):
        for u in range(UNROLL):
            q = j * UNROLL + u
            a = table[pl.ds(first[base + q], 1), :]
            b = table[pl.ds(second[base + q], 1), :]
            buf[pl.ds(q, 1), :] = jnp.where(low, a, b)

    lax.fori_loop(0, rows // UNROLL, group, None)


def outward_kernel(
    n_narrow, n_region, first, second, feats, names, grads, weight,
    got, got_names, table,
    center, w, block, buf, faces, left, right, top, bottom, corners, stack,
    send, recv, name_send, name_recv, halo_send, halo_recv,
):
    devices = n_narrow * n_region
    me = lax.axis_index("narrow") * n_region + lax.axis_index("region")
    half = buf.shape[0]
    f32 = jnp.float32
    met = greet_all(devices, n_region, me)
    zero = jnp.zeros((NZ, 64), f32)

    def pairs(x, _):
        for k in range(PAIRS):
            a = grads[x, 2 * k - 1].astype(f32) if k > 0 else zero
            b = grads[x, 2 * k].astype(f32) if k < PAIRS - 1 else zero
            center[x, k] = jnp.concatenate([a, b], axis=1).astype(jnp.bfloat16)

    lax.fori_loop(0, center.shape[0], pairs, None)
    met()
    moves = halo_moves(
        n_narrow, n_region, center, faces, left, right, top, bottom, corners, halo_send, halo_recv
    )
    start_halo(moves, center, faces)

    def fill(ref, at, other):
        paired_rows(first, second, feats, other * half, half, buf)
        ref[at] = buf[...].astype(jnp.bfloat16)

    arrive = to_each(
        devices, n_region, me, lambda o: block.at[o], got.at[me], send, recv, lambda o: fill(block, o, o)
    )
    named = to_each(
        devices, n_region, me, lambda o: names.at[o], got_names.at[me], name_send, name_recv
    )
    fill(got, me, me)
    got_names[me] = names[me]
    stack_inside(stack, center)
    wait_halo(moves)
    stack_edges(stack, center, left, right, top, bottom, corners)
    rows = (PAIRS - 1) * NZ
    spread_weights(
        w, lambda a, b, d: weight[8 - 3 * a - b, :, pl.ds(0, 192)].astype(f32)[:, 128 - d * 64 : 192 - d * 64]
    )

    def emit(xp, total):
        for i in range(2):
            at = pl.multiple_of((2 * xp + i) * rows, rows)
            table[pl.ds(at, rows), :] = total[:, i * 128 : (i + 1) * 128].astype(jnp.bfloat16)

    convolve(stack, w, emit)
    arrive()
    named()


def splat_kernel(devices, slots, from_ref, to_ref, got_ref, cells_ref, buf, *sums):
    half = slots // 2
    rows = devices * half
    f32 = jnp.float32
    low = low_lanes(half)

    def load(s, _):
        t = got_ref[s].astype(f32)
        a, b = jnp.where(low, t, 0.0), jnp.where(low, 0.0, t)
        at = pl.multiple_of(s * half, half)
        for i, form in enumerate((a, swapped(a), swapped(b), b)):
            buf[pl.ds(i * rows + at, half), :] = form

    lax.fori_loop(0, devices, load, None)
    rows_x, pairs = cells_ref.shape[:2]
    span = pairs * NZ

    def clear(x, _):
        for each in sums:
            each[pl.ds(pl.multiple_of(x * span, span), span), :] = jnp.zeros((span, 128), f32)

    lax.fori_loop(0, rows_x, clear, None)

    def visits(j, _):
        for u in range(0, VISITS, len(sums)):
            k = j * VISITS + u
            at = [pl.ds(to_ref[k + i], 1) for i in range(len(sums))]
            new = [
                each[at[i], :] + buf[pl.ds(from_ref[k + i], 1), :] for i, each in enumerate(sums)
            ]
            for i, each in enumerate(sums):
                each[at[i], :] = new[i]

    lax.fori_loop(0, devices * slots // VISITS, visits, None)

    def finish(x, _):
        for k in range(pairs):
            at = pl.ds(pl.multiple_of(x * span + k * NZ, NZ), NZ)
            total = sums[0][at, :]
            for each in sums[1:]:
                total += each[at, :]
            cells_ref[x, k] = total.astype(jnp.bfloat16)

    lax.fori_loop(0, rows_x, finish, None)


def inward_kernel(
    n_narrow, n_region, scale, first, second, collect, packed_table, center, cot, weight,
    result, point_out, weight_out,
    w, grads, planes, table, block, back, buf, faces, left, right, top, bottom, corners, stack,
    products, kernels, parts, mine, rows_buf, out_buf,
    send, recv, halo_send, halo_recv, part_send, part_recv, all_send, all_recv,
):
    devices = n_narrow * n_region
    me = lax.axis_index("narrow") * n_region + lax.axis_index("region")
    half = buf.shape[0]
    f32, bf16 = jnp.float32, jnp.bfloat16
    low = low_lanes(NZ)
    rows_x = center.shape[0]
    met = greet_all(devices, n_region, me)
    spread_weights(w, lambda a, b, d: weight[3 * a + b, pl.ds(d * 64, 64), :].astype(f32))
    met()
    moves = halo_moves(
        n_narrow, n_region, center, faces, left, right, top, bottom, corners, halo_send, halo_recv
    )
    start_halo(moves, center, faces)

    def widen(t, _):
        u = packed_table[pl.ds(pl.multiple_of(t * NZ, NZ), NZ), :].astype(f32)
        v = swapped(u)
        at = pl.multiple_of(t * 2 * NZ, 2 * NZ)
        table[pl.ds(at, NZ), :] = jnp.where(low, u, v)
        table[pl.ds(at + NZ, NZ), :] = jnp.where(low, v, u)

    lax.fori_loop(0, packed_table.shape[0] // NZ, widen, None)

    def fill(ref, at, other):
        paired_rows(first, second, table, other * half, half, buf)
        ref[at] = buf[...].astype(bf16)

    arrive = to_each(
        devices, n_region, me, lambda o: block.at[o], back.at[me], send, recv, lambda o: fill(block, o, o)
    )
    fill(back, me, me)
    span = (PAIRS - 1) * NZ
    outs = cot.shape[0]

    def lay(o, _):
        for j in range(CY // 2):
            t = cot[o, :, pl.ds(j * 128, 128)].astype(f32)
            planes[j, pl.ds(pl.multiple_of(o * rows_x, 8), rows_x), :] = t

    lax.fori_loop(0, outs, lay, None)

    def turn(xp, _):
        for i in range(2):
            some = pl.ds(2 * xp + i, outs, stride=rows_x)
            for m in range(2):
                a, b = planes[2 * m, some, :], planes[2 * m + 1, some, :]
                at = pl.ds(pl.multiple_of(xp * span + m * 128, 128), 128)
                grads[pl.ds(2 * i * 64, 64), at] = jnp.where(low, a, swapped(b)).astype(bf16)
                grads[pl.ds((2 * i + 1) * 64, 64), at] = jnp.where(low, swapped(a), b).astype(bf16)

    lax.fori_loop(0, rows_x // 2, turn, None)
    stack_inside(stack, center)
    wait_halo(moves)
    stack_edges(stack, center, left, right, top, bottom, corners)

    def product(t, _):
        total = None
        for xp in range(rows_x // 2):
            here = grads[:, pl.ds(xp * span, span)]
            term = dot(here, window(stack, 2 * xp + t // 3, lax.rem(t, 3)))
            total = term if total is None else total + term
        products[t] = total

    lax.fori_loop(0, 12, product, None)

    kernels[...] = jnp.zeros_like(kernels)
    for pair in range(14):
        halves = []
        for e in range(2):
            t = 2 * pair + e
            if t >= 27:
                halves.append(jnp.zeros((64, 128), f32))
                continue
            a, b, d = t // 9, t // 3 % 3, t % 3
            value = None
            for p in range(2):
                q = b + p
                m, par = q // 2, q % 2
                some = None
                for i in range(2):
                    piece = products[(a + i) * 3 + d, pl.ds((2 * i + p) * 64, 64), pl.ds(m * 128, 128)]
                    some = piece if some is None else some + piece
                some = some if par == e else swapped(some)
                value = some if value is None else value + some
            halves.append(value)
        kernels[pl.ds(pair * 64, 64), :] = jnp.where(low, halves[0], halves[1])

    per = mine.shape[0]
    part = lambda o: kernels.at[pl.ds(pl.multiple_of(o * per, per), per)]
    parts_in = to_each(
        devices, n_region, me, part, parts.at[me], part_send, part_recv
    )
    parts[me] = kernels[pl.ds(pl.multiple_of(me * per, per), per), :]

    def emit(xp, total):
        t = total.T
        for i in range(2):
            at = pl.ds(pl.multiple_of((2 * xp + i) * 64, 64), 64)
            for m in range(2):
                a = t[i * 128 : i * 128 + 64, m * 128 : (m + 1) * 128]
                b = t[i * 128 + 64 : i * 128 + 128, m * 128 : (m + 1) * 128]
                planes[2 * m, at, :] = jnp.where(low, a, swapped(b))
                planes[2 * m + 1, at, :] = jnp.where(low, swapped(a), b)

    convolve(stack, w, emit)

    def settle(o, _):
        for j in range(CY // 2):
            t = planes[j, pl.ds(o, rows_x, stride=outs), :]
            result[o, :, pl.ds(j * 128, 128)] = t.astype(bf16)

    lax.fori_loop(0, outs, settle, None)

    parts_in()
    mine[...] = lax.fori_loop(
        1, devices, lambda s, total: total + parts[s], parts[0]
    ) * scale
    here = pl.ds(pl.multiple_of(me * per, per), per)
    gathered = to_each(
        devices, n_region, me, lambda o: mine, weight_out.at[here], all_send, all_recv
    )
    weight_out[here, :] = mine[...]

    arrive()
    rows = devices * half

    def unpack(s, _):
        t = back[s].astype(f32)
        at = pl.multiple_of(s * half, half)
        rows_buf[pl.ds(at, half), :] = t
        rows_buf[pl.ds(rows + at, half), :] = swapped(t)

    lax.fori_loop(0, devices, unpack, None)
    few = out_buf.shape[0]
    points = point_out.shape[1]
    row_low = low_lanes(1)

    def gather(j, _):
        def group(g, _):
            for u in range(UNROLL):
                q = g * UNROLL + u
                a = rows_buf[pl.ds(collect[j * few + q], 1), :]
                b = rows_buf[pl.ds(collect[points // 2 + j * few + q], 1), :]
                out_buf[pl.ds(q, 1), :] = jnp.where(row_low, a, b)

        lax.fori_loop(0, few // UNROLL, group, None)
        t = out_buf[...].T.astype(bf16)
        at = pl.multiple_of(j * few, few)
        point_out[:, pl.ds(at, few)] = t[:64]
        point_out[:, pl.ds(points // 2 + at, few)] = t[64:]

    lax.fori_loop(0, points // 2 // few, gather, None)
    gathered()


def call(kernel, out_shape, kinds, out_kinds, scratch, collective_id, cost, *operands):
    where = {"s": pltpu.SMEM, "v": pltpu.VMEM, "a": pl.ANY}
    specs = [pl.BlockSpec(memory_space=where[k]) for k in out_kinds]
    remote = {} if collective_id is None else dict(collective_id=collective_id, has_side_effects=True)
    return pl.pallas_call(
        kernel,
        out_shape=out_shape,
        in_specs=[pl.BlockSpec(memory_space=where[k]) for k in kinds],
        out_specs=specs if len(specs) > 1 else specs[0],
        scratch_shapes=scratch,
        compiler_params=pltpu.CompilerParams(vmem_limit_bytes=56 << 20, **remote),
        cost_estimate=pl.CostEstimate(flops=0, bytes_accessed=cost, transcendentals=0),
    )(*operands)


def halo_scratch(rows_x):
    bf16 = jnp.bfloat16
    side = pltpu.VMEM((rows_x // 2, NZ, 128), bf16)
    end = pltpu.VMEM((PAIRS, NZ, 128), bf16)
    return [
        pltpu.VMEM((2, rows_x // 2, NZ, 128), bf16),
        side,
        side,
        end,
        end,
        pltpu.VMEM((4, NZ, 128), bf16),
        pltpu.VMEM((rows_x + 2, 3, PAIRS * NZ, 128), bf16),
    ]


def ranks(owner, devices):
    span = 128
    chunks = owner.shape[0] // span
    marks = owner.reshape(chunks, span)[:, :, None] == jnp.arange(devices, dtype=jnp.int32)
    ones = marks.astype(jnp.bfloat16)
    before = (jnp.arange(span)[:, None] > jnp.arange(span)[None, :]).astype(jnp.bfloat16)
    inner = jnp.einsum("ij,cjo->cio", before, ones, preferred_element_type=jnp.float32)
    tallies = jnp.sum(ones.astype(jnp.float32), axis=1)
    ahead = (jnp.arange(chunks)[:, None] > jnp.arange(chunks)[None, :]).astype(jnp.bfloat16)
    starts = jnp.einsum("ij,jo->io", ahead, tallies.astype(jnp.bfloat16), preferred_element_type=jnp.float32)
    slot = jnp.sum(jnp.where(marks, inner + starts[:, None, :], 0.0), axis=2)
    return slot.reshape(-1).astype(jnp.int32), jnp.sum(tallies, axis=0).astype(jnp.int32)


def shards(point_feats, point_owner, point_voxel, weight, cotangent):
    n_narrow = lax.axis_size("narrow")
    n_region = lax.axis_size("region")
    devices = n_narrow * n_region
    chans, points_here = point_feats.shape
    slots = 2 * points_here // devices
    half = slots // 2
    rows = devices * half
    rows_x = cotangent.shape[1]
    voxels = rows_x * CY * NZ
    f32, bf16, i32 = jnp.float32, jnp.bfloat16, jnp.int32
    dma = pltpu.SemaphoreType.DMA

    grads = cotangent.reshape(chans, rows_x, CY, NZ).transpose(1, 2, 3, 0)
    weights = pltpu.VMEM((5, 3, 4 * chans, 2 * chans), bf16)

    owner = point_owner[:, 0]
    slot, sent = ranks(owner, devices)
    marks = owner[:, None] == jnp.arange(devices, dtype=i32)
    index = jnp.arange(points_here, dtype=i32)
    values = jnp.stack([index // 64, index % 64, point_voxel // 128, point_voxel % 128], axis=1)
    named = jnp.where(marks[:, None, :], values[:, :, None], 0).astype(bf16).reshape(points_here, -1)
    seats = (slot[:, None] == jnp.arange(slots, dtype=i32)).astype(bf16)
    dealt = jnp.einsum("pa,ps->as", named, seats, preferred_element_type=f32)
    dealt = dealt.reshape(4, devices, slots)
    source = (dealt[0] * 64 + dealt[1]).astype(i32)
    filled = jnp.arange(slots, dtype=i32)[None, :] < sent[:, None]
    names = jnp.where(filled, (dealt[2] * 128 + dealt[3]).astype(i32), voxels)
    wide = -(-slots // 128) * 128
    names = jnp.pad(names, ((0, 0), (0, wide - slots))).reshape(devices, wide // 128, 128)
    feats = jnp.concatenate([point_feats, point_feats], axis=0).T.astype(f32)

    got, got_names, packed_table = call(
        functools.partial(outward_kernel, n_narrow, n_region),
        (
            jax.ShapeDtypeStruct((devices, half, 2 * chans), bf16),
            jax.ShapeDtypeStruct(names.shape, i32),
            jax.ShapeDtypeStruct((voxels // 2, 2 * chans), bf16),
        ),
        "ssvvvv",
        "vvv",
        [
            pltpu.VMEM((rows_x, PAIRS, NZ, 2 * chans), bf16),
            weights,
            pltpu.VMEM((devices, half, 2 * chans), bf16),
            pltpu.VMEM((half, 2 * chans), f32),
        ]
        + halo_scratch(rows_x)
        + [dma((devices,))] * 4
        + [dma((8,)), dma((8,))],
        0,
        60 << 20,
        source[:, :half].reshape(-1),
        source[:, half:].reshape(-1),
        feats,
        names,
        grads,
        weight,
    )

    got_vox = got_names.reshape(devices, wide)[:, :slots]
    padded_y = got_vox // NZ % CY + 1
    row = (got_vox // (CY * NZ) * PAIRS + padded_y // 2) * NZ + got_vox % NZ
    there = got_vox < voxels
    add_at = jnp.where(there, row, rows_x * PAIRS * NZ)
    seats = jnp.arange(slots, dtype=i32)[None, :]
    form = 2 * (seats // half) + padded_y % 2
    add_from = form * rows + jnp.arange(devices, dtype=i32)[:, None] * half + seats % half
    pick_at = jnp.where(there, got_vox, 0)

    cells = call(
        functools.partial(splat_kernel, devices, slots),
        jax.ShapeDtypeStruct((rows_x, PAIRS, NZ, 2 * chans), bf16),
        "ssv",
        "v",
        [pltpu.VMEM((4 * rows, 2 * chans), f32)]
        + [pltpu.VMEM((rows_x * PAIRS * NZ + 8, 2 * chans), f32)] * COPIES,
        None,
        60 << 20,
        add_from.reshape(-1),
        add_at.reshape(-1),
        got,
    )

    seat = owner * half + slot % half
    side = slot // half
    wanted = index // (points_here // 2)
    collect = jnp.where(side == wanted, 0, rows) + seat
    total_cells = rows_x * n_region * CY * n_narrow * NZ
    kernel_rows = 1024
    per = kernel_rows // devices
    few = 128
    result, point_grad, kernels = call(
        functools.partial(inward_kernel, n_narrow, n_region, 1.0 / math.sqrt(total_cells)),
        (
            jax.ShapeDtypeStruct((chans, rows_x, CY * NZ), bf16),
            jax.ShapeDtypeStruct((chans, points_here), bf16),
            jax.ShapeDtypeStruct((kernel_rows, 2 * chans), f32),
        ),
        "sssvvvv",
        "vvv",
        [
            weights,
            pltpu.VMEM((4 * chans, voxels // 4), bf16),
            pltpu.VMEM((CY // 2, rows_x * chans, 2 * NZ), f32),
            pltpu.VMEM((voxels, 2 * chans), f32),
            pltpu.VMEM((devices, half, 2 * chans), bf16),
            pltpu.VMEM((devices, half, 2 * chans), bf16),
            pltpu.VMEM((half, 2 * chans), f32),
        ]
        + halo_scratch(rows_x)
        + [
            pltpu.VMEM((12, 4 * chans, 4 * chans), f32),
            pltpu.VMEM((kernel_rows, 2 * chans), f32),
            pltpu.VMEM((devices, per, 2 * chans), f32),
            pltpu.VMEM((per, 2 * chans), f32),
            pltpu.VMEM((2 * rows, 2 * chans), f32),
            pltpu.VMEM((few, 2 * chans), f32),
        ]
        + [dma((devices,)), dma((devices,)), dma((8,)), dma((8,))]
        + [dma((devices,))] * 4,
        1,
        100 << 20,
        pick_at[:, :half].reshape(-1),
        pick_at[:, half:].reshape(-1),
        collect,
        packed_table,
        cells,
        cotangent,
        weight.transpose(0, 2, 1),
    )
    kernels = kernels.reshape(kernel_rows // 64, 64, 2, 64).transpose(0, 2, 1, 3).reshape(-1, 64, 64)
    weight_grad = kernels[:27].reshape(9, 3, 64, 64).transpose(0, 2, 1, 3).reshape(9, 64, 192)
    return (result, point_grad, weight_grad)


def solution(mesh):
    in_specs = (
        P(None, AXES),
        P(AXES, None),
        P(AXES),
        P(),
        P(None, "region", "narrow"),
    )
    out_specs = (P(None, "region", "narrow"), P(None, AXES), P())
    return jax.shard_map(shards, mesh=mesh, in_specs=in_specs, out_specs=out_specs, check_vma=False)
```

```python
import functools
import math

import jax
import jax.numpy as jnp
from jax import lax
from jax.experimental import pallas as pl
from jax.experimental.pallas import tpu as pltpu
from jax.sharding import PartitionSpec as P

NZ = 64
CY = 8
AXES = ("narrow", "region")
UNROLL = 16
COPIES = 4
VISITS = 128
PAIRS = CY // 2 + 1
MESH = pl.DeviceIdType.MESH


def dot(a, b):
    return jnp.dot(a, b, preferred_element_type=jnp.float32)


def low_lanes(rows):
    return lax.broadcasted_iota(jnp.int32, (rows, 128), 1) < 64


def swapped(t):
    return pltpu.roll(t, 64, 1)


def device(flat, n_region):
    return (flat // n_region, lax.rem(flat, n_region))


def greet_all(devices, n_region, me):
    barrier = pltpu.get_barrier_semaphore()

    def greet(s, _):
        other = device(lax.rem(me + s, devices), n_region)
        pl.semaphore_signal(barrier, inc=1, device_id=other, device_id_type=MESH)

    lax.fori_loop(1, devices, greet, None)
    return lambda: pl.semaphore_wait(barrier, devices - 1)


def halo_moves(n_narrow, n_region, center, faces, left, right, top, bottom, corners, send, recv):
    n, r = lax.axis_index("narrow"), lax.axis_index("region")
    last = center.shape[0] - 1
    west, east = lax.rem(n + n_narrow - 1, n_narrow), lax.rem(n + 1, n_narrow)
    north, south = lax.rem(r + n_region - 1, n_region), lax.rem(r + 1, n_region)
    w, e, u, d = n > 0, n < n_narrow - 1, r > 0, r < n_region - 1
    both = jnp.logical_and
    table = [
        (w, e, (west, r), faces.at[0], right),
        (e, w, (east, r), faces.at[1], left),
        (u, d, (n, north), center.at[0], bottom),
        (d, u, (n, south), center.at[last], top),
        (both(w, u), both(e, d), (west, north), center.at[0, 0], corners.at[3]),
        (both(e, u), both(w, d), (east, north), center.at[0, PAIRS - 1], corners.at[2]),
        (both(w, d), both(e, u), (west, south), center.at[last, 0], corners.at[1]),
        (both(e, d), both(w, u), (east, south), center.at[last, PAIRS - 1], corners.at[0]),
    ]
    return [
        (
            sends,
            gets,
            pltpu.make_async_remote_copy(
                src_ref=source,
                dst_ref=target,
                send_sem=send.at[i],
                recv_sem=recv.at[i],
                device_id=where,
                device_id_type=MESH,
            ),
            target,
        )
        for i, (sends, gets, where, source, target) in enumerate(table)
    ]


def start_halo(moves, center, faces):
    half_x = center.shape[0] // 2
    f32 = jnp.float32

    def face(x, _):
        for i, k in ((0, 0), (1, PAIRS - 1)):
            tile = center[x, k].astype(f32) + swapped(center[x + half_x, k].astype(f32))
            faces[i, x] = tile.astype(jnp.bfloat16)

    lax.fori_loop(0, half_x, face, None)
    for sends, gets, copy, target in moves:

        @pl.when(sends)
        def _():
            copy.start()

        @pl.when(jnp.logical_not(gets))
        def _():
            target[...] = jnp.zeros(target.shape, target.dtype)


def wait_halo(moves):
    for sends, gets, copy, _ in moves:

        @pl.when(gets)
        def _():
            copy.wait_recv()

        @pl.when(sends)
        def _():
            copy.wait_send()


def put(stack, x, k, t):
    row = lax.broadcasted_iota(jnp.int32, t.shape, 0)
    at = pl.ds(k * NZ, NZ)
    up = jnp.where(row == 0, 0.0, pltpu.roll(t, 1, 0))
    down = jnp.where(row == NZ - 1, 0.0, pltpu.roll(t, NZ - 1, 0))
    stack[x, 0, at, :] = up.astype(jnp.bfloat16)
    stack[x, 1, at, :] = t.astype(jnp.bfloat16)
    stack[x, 2, at, :] = down.astype(jnp.bfloat16)


def stack_inside(stack, center):
    def plane(x, _):
        for k in range(1, PAIRS - 1):
            put(stack, x + 1, k, center[x, k].astype(jnp.float32))

    lax.fori_loop(0, center.shape[0], plane, None)


def stack_edges(stack, center, left, right, top, bottom, corners):
    rows_x = center.shape[0]
    half_x = rows_x // 2
    f32 = jnp.float32
    low = low_lanes(NZ)
    end = PAIRS - 1

    def sides(x, _):
        from_left, from_right = left[x].astype(f32), right[x].astype(f32)
        for at, l, r in (
            (x, from_left, from_right),
            (x + half_x, swapped(from_left), swapped(from_right)),
        ):
            put(stack, at + 1, 0, center[at, 0].astype(f32) + jnp.where(low, l, 0.0))
            put(stack, at + 1, end, center[at, end].astype(f32) + jnp.where(low, 0.0, r))

    lax.fori_loop(0, half_x, sides, None)
    for x, rows, c in ((0, top, 0), (rows_x + 1, bottom, 2)):
        for k in range(PAIRS):
            t = rows[k].astype(f32)
            if k == 0:
                t += corners[c].astype(f32)
            if k == end:
                t += corners[c + 1].astype(f32)
            put(stack, x, k, t)


def window(stack, x, d):
    rows = (PAIRS - 1) * NZ
    return jnp.concatenate([stack[x, d, pl.ds(0, rows), :], stack[x, d, pl.ds(NZ, rows), :]], axis=1)


def spread_weights(w, block):
    zero = jnp.zeros((64, 64), jnp.float32)
    for a in (0, 4):
        w[a] = jnp.zeros(w.shape[1:], w.dtype)
    for a in range(3):
        for d in range(3):
            for q in range(4):
                left = block(a, q, d) if q < 3 else zero
                right = block(a, q - 1, d) if q > 0 else zero
                both = jnp.concatenate([left, right], axis=1)
                w[a + 1, d, pl.ds(q * 64, 64), :] = both.astype(jnp.bfloat16)


def convolve(stack, w, emit):
    def step(xp, _):
        total = None
        for i in range(4):
            for d in range(3):
                both = jnp.concatenate([w[i + 1, d], w[i, d]], axis=1)
                term = dot(window(stack, 2 * xp + i, d), both)
                total = term if total is None else total + term
        emit(xp, total)

    lax.fori_loop(0, (stack.shape[0] - 2) // 2, step, None)


def far_first(step, devices, n_region, me):
    n_narrow = devices // n_region
    turn = step // n_narrow
    off = n_region // 2 + (turn + 1) // 2 * (1 - 2 * lax.rem(turn, 2))
    n = lax.rem(me // n_region + lax.rem(step, n_narrow) + 1, n_narrow)
    return n * n_region + lax.rem(lax.rem(me, n_region) + off, n_region)


def to_each(devices, n_region, me, source, target, send, recv, visit=None):
    def copy(s):
        other = far_first(s, devices, n_region, me)
        return pltpu.make_async_remote_copy(
            src_ref=source(other),
            dst_ref=target,
            send_sem=send.at[s],
            recv_sem=recv.at[s],
            device_id=device(other, n_region),
            device_id_type=MESH,
        )

    def go(s, _):
        if visit is not None:
            visit(far_first(s, devices, n_region, me))
        copy(s).start()

    def finish(s, _):
        copy(s).wait_recv()
        copy(s).wait_send()

    lax.fori_loop(0, devices - 1, go, None)
    return lambda: lax.fori_loop(0, devices - 1, finish, None)


def paired_rows(first, second, table, base, rows, buf):
    low = low_lanes(1)

    def group(j, _):
        for u in range(UNROLL):
            q = j * UNROLL + u
            a = table[pl.ds(first[base + q], 1), :]
            b = table[pl.ds(second[base + q], 1), :]
            buf[pl.ds(q, 1), :] = jnp.where(low, a, b)

    lax.fori_loop(0, rows // UNROLL, group, None)


def outward_kernel(
    n_narrow, n_region, first, second, feats, names, grads, weight,
    got, got_names, table,
    center, w, block, buf, faces, left, right, top, bottom, corners, stack,
    send, recv, name_send, name_recv, halo_send, halo_recv,
):
    devices = n_narrow * n_region
    me = lax.axis_index("narrow") * n_region + lax.axis_index("region")
    half = buf.shape[0]
    f32 = jnp.float32
    met = greet_all(devices, n_region, me)
    zero = jnp.zeros((NZ, 64), f32)

    def pairs(x, _):
        for k in range(PAIRS):
            a = grads[x, 2 * k - 1].astype(f32) if k > 0 else zero
            b = grads[x, 2 * k].astype(f32) if k < PAIRS - 1 else zero
            center[x, k] = jnp.concatenate([a, b], axis=1).astype(jnp.bfloat16)

    lax.fori_loop(0, center.shape[0], pairs, None)
    met()
    moves = halo_moves(
        n_narrow, n_region, center, faces, left, right, top, bottom, corners, halo_send, halo_recv
    )
    start_halo(moves, center, faces)

    def fill(ref, at, other):
        paired_rows(first, second, feats, other * half, half, buf)
        ref[at] = buf[...].astype(jnp.bfloat16)

    arrive = to_each(
        devices, n_region, me, lambda o: block.at[o], got.at[me], send, recv, lambda o: fill(block, o, o)
    )
    named = to_each(
        devices, n_region, me, lambda o: names.at[o], got_names.at[me], name_send, name_recv
    )
    fill(got, me, me)
    got_names[me] = names[me]
    stack_inside(stack, center)
    wait_halo(moves)
    stack_edges(stack, center, left, right, top, bottom, corners)
    rows = (PAIRS - 1) * NZ
    spread_weights(
        w, lambda a, b, d: weight[8 - 3 * a - b, :, pl.ds(0, 192)].astype(f32)[:, 128 - d * 64 : 192 - d * 64]
    )

    def emit(xp, total):
        for i in range(2):
            at = pl.multiple_of((2 * xp + i) * rows, rows)
            table[pl.ds(at, rows), :] = total[:, i * 128 : (i + 1) * 128].astype(jnp.bfloat16)

    convolve(stack, w, emit)
    arrive()
    named()


def splat_kernel(devices, slots, from_ref, to_ref, got_ref, cells_ref, buf, *sums):
    half = slots // 2
    rows = devices * half
    f32 = jnp.float32
    low = low_lanes(half)

    def load(s, _):
        t = got_ref[s].astype(f32)
        a, b = jnp.where(low, t, 0.0), jnp.where(low, 0.0, t)
        at = pl.multiple_of(s * half, half)
        for i, form in enumerate((a, swapped(a), swapped(b), b)):
            buf[pl.ds(i * rows + at, half), :] = form

    lax.fori_loop(0, devices, load, None)
    rows_x, pairs = cells_ref.shape[:2]
    span = pairs * NZ

    def clear(x, _):
        for each in sums:
            each[pl.ds(pl.multiple_of(x * span, span), span), :] = jnp.zeros((span, 128), f32)

    lax.fori_loop(0, rows_x, clear, None)

    def visits(j, _):
        for u in range(0, VISITS, len(sums)):
            k = j * VISITS + u
            at = [pl.ds(to_ref[k + i], 1) for i in range(len(sums))]
            new = [
                each[at[i], :] + buf[pl.ds(from_ref[k + i], 1), :] for i, each in enumerate(sums)
            ]
            for i, each in enumerate(sums):
                each[at[i], :] = new[i]

    lax.fori_loop(0, devices * slots // VISITS, visits, None)

    def finish(x, _):
        for k in range(pairs):
            at = pl.ds(pl.multiple_of(x * span + k * NZ, NZ), NZ)
            total = sums[0][at, :]
            for each in sums[1:]:
                total += each[at, :]
            cells_ref[x, k] = total.astype(jnp.bfloat16)

    lax.fori_loop(0, rows_x, finish, None)


def inward_kernel(
    n_narrow, n_region, scale, first, second, collect, packed_table, center, cot, weight,
    result, point_out, weight_out,
    w, grads, planes, table, block, back, buf, faces, left, right, top, bottom, corners, stack,
    products, kernels, parts, mine, sums, rows_buf, out_buf,
    send, recv, halo_send, halo_recv, part_send, part_recv, all_send, all_recv,
):
    devices = n_narrow * n_region
    me = lax.axis_index("narrow") * n_region + lax.axis_index("region")
    half = buf.shape[0]
    f32, bf16 = jnp.float32, jnp.bfloat16
    low = low_lanes(NZ)
    rows_x = center.shape[0]
    met = greet_all(devices, n_region, me)
    spread_weights(w, lambda a, b, d: weight[3 * a + b, pl.ds(d * 64, 64), :].astype(f32))
    met()
    moves = halo_moves(
        n_narrow, n_region, center, faces, left, right, top, bottom, corners, halo_send, halo_recv
    )
    start_halo(moves, center, faces)

    def widen(t, _):
        u = packed_table[pl.ds(pl.multiple_of(t * NZ, NZ), NZ), :].astype(f32)
        v = swapped(u)
        at = pl.multiple_of(t * 2 * NZ, 2 * NZ)
        table[pl.ds(at, NZ), :] = jnp.where(low, u, v)
        table[pl.ds(at + NZ, NZ), :] = jnp.where(low, v, u)

    lax.fori_loop(0, packed_table.shape[0] // NZ, widen, None)

    def fill(ref, at, other):
        paired_rows(first, second, table, other * half, half, buf)
        ref[at] = buf[...].astype(bf16)

    arrive = to_each(
        devices, n_region, me, lambda o: block.at[o], back.at[me], send, recv, lambda o: fill(block, o, o)
    )
    fill(back, me, me)
    span = (PAIRS - 1) * NZ
    outs = cot.shape[0]

    def lay(o, _):
        for j in range(CY // 2):
            t = cot[o, :, pl.ds(j * 128, 128)].astype(f32)
            planes[j, pl.ds(pl.multiple_of(o * rows_x, 8), rows_x), :] = t

    lax.fori_loop(0, outs, lay, None)

    def turn(xp, _):
        for i in range(2):
            some = pl.ds(2 * xp + i, outs, stride=rows_x)
            for m in range(2):
                a, b = planes[2 * m, some, :], planes[2 * m + 1, some, :]
                at = pl.ds(pl.multiple_of(xp * span + m * 128, 128), 128)
                grads[pl.ds(2 * i * 64, 64), at] = jnp.where(low, a, swapped(b)).astype(bf16)
                grads[pl.ds((2 * i + 1) * 64, 64), at] = jnp.where(low, swapped(a), b).astype(bf16)

    lax.fori_loop(0, rows_x // 2, turn, None)
    stack_inside(stack, center)
    wait_halo(moves)
    stack_edges(stack, center, left, right, top, bottom, corners)

    def product(t, _):
        total = None
        for xp in range(rows_x // 2):
            here = grads[:, pl.ds(xp * span, span)]
            term = dot(here, window(stack, 2 * xp + t // 3, lax.rem(t, 3)))
            total = term if total is None else total + term
        products[t] = total

    lax.fori_loop(0, 12, product, None)

    kernels[...] = jnp.zeros_like(kernels)
    for pair in range(14):
        halves = []
        for e in range(2):
            t = 2 * pair + e
            if t >= 27:
                halves.append(jnp.zeros((64, 128), f32))
                continue
            a, b, d = t // 9, t // 3 % 3, t % 3
            value = None
            for p in range(2):
                q = b + p
                m, par = q // 2, q % 2
                some = None
                for i in range(2):
                    piece = products[(a + i) * 3 + d, pl.ds((2 * i + p) * 64, 64), pl.ds(m * 128, 128)]
                    some = piece if some is None else some + piece
                some = some if par == e else swapped(some)
                value = some if value is None else value + some
            halves.append(value)
        kernels[pl.ds(pair * 64, 64), :] = jnp.where(low, halves[0], halves[1])

    per = mine.shape[0]
    part = lambda o: kernels.at[pl.ds(pl.multiple_of(o * per, per), per)]
    parts_in = to_each(
        devices, n_region, me, part, parts.at[me], part_send, part_recv
    )
    parts[me] = kernels[pl.ds(pl.multiple_of(me * per, per), per), :]

    def emit(xp, total):
        t = total.T
        for i in range(2):
            at = pl.ds(pl.multiple_of((2 * xp + i) * 64, 64), 64)
            for m in range(2):
                a = t[i * 128 : i * 128 + 64, m * 128 : (m + 1) * 128]
                b = t[i * 128 + 64 : i * 128 + 128, m * 128 : (m + 1) * 128]
                planes[2 * m, at, :] = jnp.where(low, a, swapped(b))
                planes[2 * m + 1, at, :] = jnp.where(low, swapped(a), b)

    convolve(stack, w, emit)

    def settle(o, _):
        for j in range(CY // 2):
            t = planes[j, pl.ds(o, rows_x, stride=outs), :]
            result[o, :, pl.ds(j * 128, 128)] = t.astype(bf16)

    lax.fori_loop(0, outs, settle, None)

    parts_in()
    total = lax.fori_loop(1, devices, lambda s, total: total + parts[s], parts[0])
    mine[...] = (total * scale).astype(bf16)
    gathered = to_each(
        devices, n_region, me, lambda o: mine, sums.at[me], all_send, all_recv
    )
    sums[me] = mine[...]

    arrive()
    rows = devices * half

    def unpack(s, _):
        t = back[s].astype(f32)
        at = pl.multiple_of(s * half, half)
        rows_buf[pl.ds(at, half), :] = t
        rows_buf[pl.ds(rows + at, half), :] = swapped(t)

    lax.fori_loop(0, devices, unpack, None)
    few = out_buf.shape[0]
    points = point_out.shape[1]
    row_low = low_lanes(1)

    def gather(j, _):
        def group(g, _):
            for u in range(UNROLL):
                q = g * UNROLL + u
                a = rows_buf[pl.ds(collect[j * few + q], 1), :]
                b = rows_buf[pl.ds(collect[points // 2 + j * few + q], 1), :]
                out_buf[pl.ds(q, 1), :] = jnp.where(row_low, a, b)

        lax.fori_loop(0, few // UNROLL, group, None)
        t = out_buf[...].T.astype(bf16)
        at = pl.multiple_of(j * few, few)
        point_out[:, pl.ds(at, few)] = t[:64]
        point_out[:, pl.ds(points // 2 + at, few)] = t[64:]

    lax.fori_loop(0, points // 2 // few, gather, None)
    gathered()

    def widen_sums(s, _):
        weight_out[pl.ds(pl.multiple_of(s * per, per), per), :] = sums[s].astype(f32)

    lax.fori_loop(0, devices, widen_sums, None)


def call(kernel, out_shape, kinds, out_kinds, scratch, collective_id, cost, *operands):
    where = {"s": pltpu.SMEM, "v": pltpu.VMEM, "a": pl.ANY}
    specs = [pl.BlockSpec(memory_space=where[k]) for k in out_kinds]
    remote = {} if collective_id is None else dict(collective_id=collective_id, has_side_effects=True)
    return pl.pallas_call(
        kernel,
        out_shape=out_shape,
        in_specs=[pl.BlockSpec(memory_space=where[k]) for k in kinds],
        out_specs=specs if len(specs) > 1 else specs[0],
        scratch_shapes=scratch,
        compiler_params=pltpu.CompilerParams(vmem_limit_bytes=56 << 20, **remote),
        cost_estimate=pl.CostEstimate(flops=0, bytes_accessed=cost, transcendentals=0),
    )(*operands)


def halo_scratch(rows_x):
    bf16 = jnp.bfloat16
    side = pltpu.VMEM((rows_x // 2, NZ, 128), bf16)
    end = pltpu.VMEM((PAIRS, NZ, 128), bf16)
    return [
        pltpu.VMEM((2, rows_x // 2, NZ, 128), bf16),
        side,
        side,
        end,
        end,
        pltpu.VMEM((4, NZ, 128), bf16),
        pltpu.VMEM((rows_x + 2, 3, PAIRS * NZ, 128), bf16),
    ]


def ranks(owner, devices):
    span = 128
    chunks = owner.shape[0] // span
    marks = owner.reshape(chunks, span)[:, :, None] == jnp.arange(devices, dtype=jnp.int32)
    ones = marks.astype(jnp.bfloat16)
    before = (jnp.arange(span)[:, None] > jnp.arange(span)[None, :]).astype(jnp.bfloat16)
    inner = jnp.einsum("ij,cjo->cio", before, ones, preferred_element_type=jnp.float32)
    tallies = jnp.sum(ones.astype(jnp.float32), axis=1)
    ahead = (jnp.arange(chunks)[:, None] > jnp.arange(chunks)[None, :]).astype(jnp.bfloat16)
    starts = jnp.einsum("ij,jo->io", ahead, tallies.astype(jnp.bfloat16), preferred_element_type=jnp.float32)
    slot = jnp.sum(jnp.where(marks, inner + starts[:, None, :], 0.0), axis=2)
    return slot.reshape(-1).astype(jnp.int32), jnp.sum(tallies, axis=0).astype(jnp.int32)


def shards(point_feats, point_owner, point_voxel, weight, cotangent):
    n_narrow = lax.axis_size("narrow")
    n_region = lax.axis_size("region")
    devices = n_narrow * n_region
    chans, points_here = point_feats.shape
    slots = 2 * points_here // devices
    half = slots // 2
    rows = devices * half
    rows_x = cotangent.shape[1]
    voxels = rows_x * CY * NZ
    f32, bf16, i32 = jnp.float32, jnp.bfloat16, jnp.int32
    dma = pltpu.SemaphoreType.DMA

    grads = cotangent.reshape(chans, rows_x, CY, NZ).transpose(1, 2, 3, 0)
    weights = pltpu.VMEM((5, 3, 4 * chans, 2 * chans), bf16)

    owner = point_owner[:, 0]
    slot, sent = ranks(owner, devices)
    marks = owner[:, None] == jnp.arange(devices, dtype=i32)
    index = jnp.arange(points_here, dtype=i32)
    values = jnp.stack([index // 64, index % 64, point_voxel // 128, point_voxel % 128], axis=1)
    named = jnp.where(marks[:, None, :], values[:, :, None], 0).astype(bf16).reshape(points_here, -1)
    seats = (slot[:, None] == jnp.arange(slots, dtype=i32)).astype(bf16)
    dealt = jnp.einsum("pa,ps->as", named, seats, preferred_element_type=f32)
    dealt = dealt.reshape(4, devices, slots)
    source = (dealt[0] * 64 + dealt[1]).astype(i32)
    filled = jnp.arange(slots, dtype=i32)[None, :] < sent[:, None]
    names = jnp.where(filled, (dealt[2] * 128 + dealt[3]).astype(i32), voxels)
    wide = -(-slots // 128) * 128
    names = jnp.pad(names, ((0, 0), (0, wide - slots))).reshape(devices, wide // 128, 128)
    feats = jnp.concatenate([point_feats, point_feats], axis=0).T.astype(f32)

    got, got_names, packed_table = call(
        functools.partial(outward_kernel, n_narrow, n_region),
        (
            jax.ShapeDtypeStruct((devices, half, 2 * chans), bf16),
            jax.ShapeDtypeStruct(names.shape, i32),
            jax.ShapeDtypeStruct((voxels // 2, 2 * chans), bf16),
        ),
        "ssvvvv",
        "vvv",
        [
            pltpu.VMEM((rows_x, PAIRS, NZ, 2 * chans), bf16),
            weights,
            pltpu.VMEM((devices, half, 2 * chans), bf16),
            pltpu.VMEM((half, 2 * chans), f32),
        ]
        + halo_scratch(rows_x)
        + [dma((devices,))] * 4
        + [dma((8,)), dma((8,))],
        0,
        60 << 20,
        source[:, :half].reshape(-1),
        source[:, half:].reshape(-1),
        feats,
        names,
        grads,
        weight,
    )

    got_vox = got_names.reshape(devices, wide)[:, :slots]
    padded_y = got_vox // NZ % CY + 1
    row = (got_vox // (CY * NZ) * PAIRS + padded_y // 2) * NZ + got_vox % NZ
    there = got_vox < voxels
    add_at = jnp.where(there, row, rows_x * PAIRS * NZ)
    seats = jnp.arange(slots, dtype=i32)[None, :]
    form = 2 * (seats // half) + padded_y % 2
    add_from = form * rows + jnp.arange(devices, dtype=i32)[:, None] * half + seats % half
    pick_at = jnp.where(there, got_vox, 0)

    cells = call(
        functools.partial(splat_kernel, devices, slots),
        jax.ShapeDtypeStruct((rows_x, PAIRS, NZ, 2 * chans), bf16),
        "ssv",
        "v",
        [pltpu.VMEM((4 * rows, 2 * chans), f32)]
        + [pltpu.VMEM((rows_x * PAIRS * NZ + 8, 2 * chans), f32)] * COPIES,
        None,
        60 << 20,
        add_from.reshape(-1),
        add_at.reshape(-1),
        got,
    )

    seat = owner * half + slot % half
    side = slot // half
    wanted = index // (points_here // 2)
    collect = jnp.where(side == wanted, 0, rows) + seat
    total_cells = rows_x * n_region * CY * n_narrow * NZ
    kernel_rows = 1024
    per = kernel_rows // devices
    few = 128
    result, point_grad, kernels = call(
        functools.partial(inward_kernel, n_narrow, n_region, 1.0 / math.sqrt(total_cells)),
        (
            jax.ShapeDtypeStruct((chans, rows_x, CY * NZ), bf16),
            jax.ShapeDtypeStruct((chans, points_here), bf16),
            jax.ShapeDtypeStruct((kernel_rows, 2 * chans), f32),
        ),
        "sssvvvv",
        "vvv",
        [
            weights,
            pltpu.VMEM((4 * chans, voxels // 4), bf16),
            pltpu.VMEM((CY // 2, rows_x * chans, 2 * NZ), f32),
            pltpu.VMEM((voxels, 2 * chans), f32),
            pltpu.VMEM((devices, half, 2 * chans), bf16),
            pltpu.VMEM((devices, half, 2 * chans), bf16),
            pltpu.VMEM((half, 2 * chans), f32),
        ]
        + halo_scratch(rows_x)
        + [
            pltpu.VMEM((12, 4 * chans, 4 * chans), f32),
            pltpu.VMEM((kernel_rows, 2 * chans), f32),
            pltpu.VMEM((devices, per, 2 * chans), f32),
            pltpu.VMEM((per, 2 * chans), bf16),
            pltpu.VMEM((devices, per, 2 * chans), bf16),
            pltpu.VMEM((2 * rows, 2 * chans), f32),
            pltpu.VMEM((few, 2 * chans), f32),
        ]
        + [dma((devices,)), dma((devices,)), dma((8,)), dma((8,))]
        + [dma((devices,))] * 4,
        1,
        100 << 20,
        pick_at[:, :half].reshape(-1),
        pick_at[:, half:].reshape(-1),
        collect,
        packed_table,
        cells,
        cotangent,
        weight.transpose(0, 2, 1),
    )
    kernels = kernels.reshape(kernel_rows // 64, 64, 2, 64).transpose(0, 2, 1, 3).reshape(-1, 64, 64)
    weight_grad = kernels[:27].reshape(9, 3, 64, 64).transpose(0, 2, 1, 3).reshape(9, 64, 192)
    return (result, point_grad, weight_grad)


def solution(mesh):
    in_specs = (
        P(None, AXES),
        P(AXES, None),
        P(AXES),
        P(),
        P(None, "region", "narrow"),
    )
    out_specs = (P(None, "region", "narrow"), P(None, AXES), P())
    return jax.shard_map(shards, mesh=mesh, in_specs=in_specs, out_specs=out_specs, check_vma=False)
```

```python
import functools
import math

import jax
import jax.numpy as jnp
from jax import lax
from jax.experimental import pallas as pl
from jax.experimental.pallas import tpu as pltpu
from jax.sharding import PartitionSpec as P

NZ = 64
CY = 8
AXES = ("narrow", "region")
UNROLL = 32
COPIES = 4
VISITS = 128
PAIRS = CY // 2 + 1
MESH = pl.DeviceIdType.MESH


def dot(a, b):
    return jnp.dot(a, b, preferred_element_type=jnp.float32)


def low_lanes(rows):
    return lax.broadcasted_iota(jnp.int32, (rows, 128), 1) < 64


def swapped(t):
    return pltpu.roll(t, 64, 1)


def device(flat, n_region):
    return (flat // n_region, lax.rem(flat, n_region))


def greet_all(devices, n_region, me):
    barrier = pltpu.get_barrier_semaphore()

    def greet(s, _):
        other = device(lax.rem(me + s, devices), n_region)
        pl.semaphore_signal(barrier, inc=1, device_id=other, device_id_type=MESH)

    lax.fori_loop(1, devices, greet, None)
    return lambda: pl.semaphore_wait(barrier, devices - 1)


def halo_moves(n_narrow, n_region, center, faces, left, right, top, bottom, corners, send, recv):
    n, r = lax.axis_index("narrow"), lax.axis_index("region")
    last = center.shape[0] - 1
    west, east = lax.rem(n + n_narrow - 1, n_narrow), lax.rem(n + 1, n_narrow)
    north, south = lax.rem(r + n_region - 1, n_region), lax.rem(r + 1, n_region)
    w, e, u, d = n > 0, n < n_narrow - 1, r > 0, r < n_region - 1
    both = jnp.logical_and
    table = [
        (w, e, (west, r), faces.at[0], right),
        (e, w, (east, r), faces.at[1], left),
        (u, d, (n, north), center.at[0], bottom),
        (d, u, (n, south), center.at[last], top),
        (both(w, u), both(e, d), (west, north), center.at[0, 0], corners.at[3]),
        (both(e, u), both(w, d), (east, north), center.at[0, PAIRS - 1], corners.at[2]),
        (both(w, d), both(e, u), (west, south), center.at[last, 0], corners.at[1]),
        (both(e, d), both(w, u), (east, south), center.at[last, PAIRS - 1], corners.at[0]),
    ]
    return [
        (
            sends,
            gets,
            pltpu.make_async_remote_copy(
                src_ref=source,
                dst_ref=target,
                send_sem=send.at[i],
                recv_sem=recv.at[i],
                device_id=where,
                device_id_type=MESH,
            ),
            target,
        )
        for i, (sends, gets, where, source, target) in enumerate(table)
    ]


def start_halo(moves, center, faces):
    half_x = center.shape[0] // 2
    f32 = jnp.float32

    def face(x, _):
        for i, k in ((0, 0), (1, PAIRS - 1)):
            tile = center[x, k].astype(f32) + swapped(center[x + half_x, k].astype(f32))
            faces[i, x] = tile.astype(jnp.bfloat16)

    lax.fori_loop(0, half_x, face, None)
    for sends, gets, copy, target in moves:

        @pl.when(sends)
        def _():
            copy.start()

        @pl.when(jnp.logical_not(gets))
        def _():
            target[...] = jnp.zeros(target.shape, target.dtype)


def wait_halo(moves):
    for sends, gets, copy, _ in moves:

        @pl.when(gets)
        def _():
            copy.wait_recv()

        @pl.when(sends)
        def _():
            copy.wait_send()


def put(stack, x, k, t):
    row = lax.broadcasted_iota(jnp.int32, t.shape, 0)
    at = pl.ds(k * NZ, NZ)
    up = jnp.where(row == 0, 0.0, pltpu.roll(t, 1, 0))
    down = jnp.where(row == NZ - 1, 0.0, pltpu.roll(t, NZ - 1, 0))
    stack[x, 0, at, :] = up.astype(jnp.bfloat16)
    stack[x, 1, at, :] = t.astype(jnp.bfloat16)
    stack[x, 2, at, :] = down.astype(jnp.bfloat16)


def stack_inside(stack, center):
    def plane(x, _):
        for k in range(1, PAIRS - 1):
            put(stack, x + 1, k, center[x, k].astype(jnp.float32))

    lax.fori_loop(0, center.shape[0], plane, None)


def stack_edges(stack, center, left, right, top, bottom, corners):
    rows_x = center.shape[0]
    half_x = rows_x // 2
    f32 = jnp.float32
    low = low_lanes(NZ)
    end = PAIRS - 1

    def sides(x, _):
        from_left, from_right = left[x].astype(f32), right[x].astype(f32)
        for at, l, r in (
            (x, from_left, from_right),
            (x + half_x, swapped(from_left), swapped(from_right)),
        ):
            put(stack, at + 1, 0, center[at, 0].astype(f32) + jnp.where(low, l, 0.0))
            put(stack, at + 1, end, center[at, end].astype(f32) + jnp.where(low, 0.0, r))

    lax.fori_loop(0, half_x, sides, None)
    for x, rows, c in ((0, top, 0), (rows_x + 1, bottom, 2)):
        for k in range(PAIRS):
            t = rows[k].astype(f32)
            if k == 0:
                t += corners[c].astype(f32)
            if k == end:
                t += corners[c + 1].astype(f32)
            put(stack, x, k, t)


def window(stack, x, d):
    rows = (PAIRS - 1) * NZ
    return jnp.concatenate([stack[x, d, pl.ds(0, rows), :], stack[x, d, pl.ds(NZ, rows), :]], axis=1)


def spread_weights(w, block):
    zero = jnp.zeros((64, 64), jnp.float32)
    for a in (0, 4):
        w[a] = jnp.zeros(w.shape[1:], w.dtype)
    for a in range(3):
        for d in range(3):
            for q in range(4):
                left = block(a, q, d) if q < 3 else zero
                right = block(a, q - 1, d) if q > 0 else zero
                both = jnp.concatenate([left, right], axis=1)
                w[a + 1, d, pl.ds(q * 64, 64), :] = both.astype(jnp.bfloat16)


def convolve(stack, w, emit, first, last):
    def step(xp, _):
        total = None
        for i in range(4):
            for d in range(3):
                both = jnp.concatenate([w[i + 1, d], w[i, d]], axis=1)
                term = dot(window(stack, 2 * xp + i, d), both)
                total = term if total is None else total + term
        emit(xp, total)

    lax.fori_loop(first, last, step, None)


def far_first(step, devices, n_region, me):
    n_narrow = devices // n_region
    turn = step // n_narrow
    off = n_region // 2 + (turn + 1) // 2 * (1 - 2 * lax.rem(turn, 2))
    n = lax.rem(me // n_region + lax.rem(step, n_narrow) + 1, n_narrow)
    return n * n_region + lax.rem(lax.rem(me, n_region) + off, n_region)


def to_each(devices, n_region, me, source, target, send, recv, visit=None, where=device):
    def copy(s):
        other = far_first(s, devices, n_region, me)
        return pltpu.make_async_remote_copy(
            src_ref=source(other),
            dst_ref=target,
            send_sem=send.at[s],
            recv_sem=recv.at[s],
            device_id=where(other, n_region),
            device_id_type=MESH,
        )

    def go(s, _):
        if visit is not None:
            visit(far_first(s, devices, n_region, me))
        copy(s).start()

    def finish(s, _):
        copy(s).wait_recv()
        copy(s).wait_send()

    lax.fori_loop(0, devices - 1, go, None)
    return lambda: lax.fori_loop(0, devices - 1, finish, None)


def paired_rows(first, second, table, base, rows, buf):
    low = low_lanes(1)

    def group(j, _):
        for u in range(UNROLL):
            q = j * UNROLL + u
            a = table[pl.ds(first[base + q], 1), :]
            b = table[pl.ds(second[base + q], 1), :]
            buf[pl.ds(q, 1), :] = jnp.where(low, a, b)

    lax.fori_loop(0, rows // UNROLL, group, None)


def outward_kernel(
    n_narrow, n_region, first, second, feats, names, grads, weight, far_cot,
    got, got_names, table, turned,
    planes, cot, cot_sem, center, w, block, buf, faces, left, right, top, bottom, corners, stack,
    send, recv, name_send, name_recv, halo_send, halo_recv,
):
    devices = n_narrow * n_region
    me = lax.axis_index("narrow") * n_region + lax.axis_index("region")
    half = buf.shape[0]
    f32 = jnp.float32
    bf16 = jnp.bfloat16
    fetch = pltpu.make_async_copy(far_cot, cot, cot_sem)
    fetch.start()
    met = greet_all(devices, n_region, me)
    zero = jnp.zeros((NZ, 64), f32)

    def pairs(x, _):
        for k in range(PAIRS):
            a = grads[x, 2 * k - 1].astype(f32) if k > 0 else zero
            b = grads[x, 2 * k].astype(f32) if k < PAIRS - 1 else zero
            center[x, k] = jnp.concatenate([a, b], axis=1).astype(jnp.bfloat16)

    lax.fori_loop(0, center.shape[0], pairs, None)
    met()
    moves = halo_moves(
        n_narrow, n_region, center, faces, left, right, top, bottom, corners, halo_send, halo_recv
    )
    start_halo(moves, center, faces)

    def fill(ref, at, other):
        paired_rows(first, second, feats, other * half, half, buf)
        ref[at] = buf[...].astype(jnp.bfloat16)

    arrive = to_each(
        devices, n_region, me, lambda o: block.at[o], got.at[me], send, recv, lambda o: fill(block, o, o)
    )
    named = to_each(
        devices, n_region, me, lambda o: names.at[o], got_names.at[me], name_send, name_recv
    )
    fill(got, me, me)
    got_names[me] = names[me]
    span = (PAIRS - 1) * NZ
    outs, rows_x = cot.shape[:2]
    low = low_lanes(NZ)
    fetch.wait()

    def lay(o, _):
        for j in range(CY // 2):
            t = cot[o, :, pl.ds(j * 128, 128)].astype(f32)
            planes[j, pl.ds(pl.multiple_of(o * rows_x, 8), rows_x), :] = t

    lax.fori_loop(0, outs, lay, None)

    def turn(xp, _):
        for i in range(2):
            some = pl.ds(2 * xp + i, outs, stride=rows_x)
            for m in range(2):
                a, b = planes[2 * m, some, :], planes[2 * m + 1, some, :]
                at = pl.ds(pl.multiple_of(xp * span + m * 128, 128), 128)
                turned[pl.ds(2 * i * 64, 64), at] = jnp.where(low, a, swapped(b)).astype(bf16)
                turned[pl.ds((2 * i + 1) * 64, 64), at] = jnp.where(low, swapped(a), b).astype(bf16)

    lax.fori_loop(0, rows_x // 2, turn, None)
    stack_inside(stack, center)
    wait_halo(moves)
    stack_edges(stack, center, left, right, top, bottom, corners)
    rows = (PAIRS - 1) * NZ
    spread_weights(
        w, lambda a, b, d: weight[8 - 3 * a - b, :, pl.ds(0, 192)].astype(f32)[:, 128 - d * 64 : 192 - d * 64]
    )

    def emit(xp, total):
        for i in range(2):
            at = pl.multiple_of((2 * xp + i) * rows, rows)
            table[pl.ds(at, rows), :] = total[:, i * 128 : (i + 1) * 128].astype(jnp.bfloat16)

    convolve(stack, w, emit, 0, rows_x // 2)
    arrive()
    named()


def splat_kernel(devices, slots, from_ref, to_ref, got_ref, cells_ref, buf, *sums):
    half = slots // 2
    rows = devices * half
    f32 = jnp.float32
    low = low_lanes(half)

    def load(s, _):
        t = got_ref[s].astype(f32)
        a, b = jnp.where(low, t, 0.0), jnp.where(low, 0.0, t)
        at = pl.multiple_of(s * half, half)
        for i, form in enumerate((a, swapped(a), swapped(b), b)):
            buf[pl.ds(i * rows + at, half), :] = form

    lax.fori_loop(0, devices, load, None)
    rows_x, pairs = cells_ref.shape[:2]
    span = pairs * NZ

    def clear(x, _):
        for each in sums:
            each[pl.ds(pl.multiple_of(x * span, span), span), :] = jnp.zeros((span, 128), f32)

    lax.fori_loop(0, rows_x, clear, None)

    def visits(j, _):
        for u in range(0, VISITS, len(sums)):
            k = j * VISITS + u
            at = [pl.ds(to_ref[k + i], 1) for i in range(len(sums))]
            new = [
                each[at[i], :] + buf[pl.ds(from_ref[k + i], 1), :] for i, each in enumerate(sums)
            ]
            for i, each in enumerate(sums):
                each[at[i], :] = new[i]

    lax.fori_loop(0, devices * slots // VISITS, visits, None)

    def finish(x, _):
        for k in range(pairs):
            at = pl.ds(pl.multiple_of(x * span + k * NZ, NZ), NZ)
            total = sums[0][at, :]
            for each in sums[1:]:
                total += each[at, :]
            cells_ref[x, k] = total.astype(jnp.bfloat16)

    lax.fori_loop(0, rows_x, finish, None)


def inward_kernel(
    n_narrow, n_region, scale, first, second, collect, packed_table, center, grads, weight,
    result, point_out, weight_out,
    w, planes, table, block, back, buf, faces, left, right, top, bottom, corners, stack,
    products, kernels, core_part, core_sum, parts, mine, sums, rows_buf, out_buf,
    send, recv, halo_send, halo_recv, core_send, core_recv, part_send, part_recv, all_send, all_recv,
):
    devices = n_narrow * n_region
    me = lax.axis_index("narrow") * n_region + lax.axis_index("region")
    half = buf.shape[0]
    f32, bf16 = jnp.float32, jnp.bfloat16
    low = low_lanes(NZ)
    rows_x = center.shape[0]
    met = greet_all(devices, n_region, me)
    met()
    moves = halo_moves(
        n_narrow, n_region, center, faces, left, right, top, bottom, corners, halo_send, halo_recv
    )
    start_halo(moves, center, faces)

    def widen(t, _):
        u = packed_table[pl.ds(pl.multiple_of(t * NZ, NZ), NZ), :].astype(f32)
        v = swapped(u)
        at = pl.multiple_of(t * 2 * NZ, 2 * NZ)
        table[pl.ds(at, NZ), :] = jnp.where(low, u, v)
        table[pl.ds(at + NZ, NZ), :] = jnp.where(low, v, u)

    lax.fori_loop(0, packed_table.shape[0] // NZ, widen, None)

    def fill(ref, at, other):
        paired_rows(first, second, table, other * half, half, buf)
        ref[at] = buf[...].astype(bf16)

    arrive = to_each(
        devices, n_region, me, lambda o: block.at[o], back.at[me], send, recv, lambda o: fill(block, o, o)
    )
    fill(back, me, me)
    spread_weights(w, lambda a, b, d: weight[3 * a + b, pl.ds(d * 64, 64), :].astype(f32))
    span = (PAIRS - 1) * NZ
    outs = weight.shape[2]
    stack_inside(stack, center)
    wait_halo(moves)
    stack_edges(stack, center, left, right, top, bottom, corners)

    def product(t, _):
        total = None
        for xp in range(rows_x // 2):
            here = grads[:, pl.ds(xp * span, span)]
            term = dot(here, window(stack, 2 * xp + t // 3, lax.rem(t, 3)))
            total = term if total is None else total + term
        products[t] = total

    lax.fori_loop(0, 12, product, None)

    kernels[...] = jnp.zeros_like(kernels)
    for pair in range(14):
        halves = []
        for e in range(2):
            t = 2 * pair + e
            if t >= 27:
                halves.append(jnp.zeros((64, 128), f32))
                continue
            a, b, d = t // 9, t // 3 % 3, t % 3
            value = None
            for p in range(2):
                q = b + p
                m, par = q // 2, q % 2
                some = None
                for i in range(2):
                    piece = products[(a + i) * 3 + d, pl.ds((2 * i + p) * 64, 64), pl.ds(m * 128, 128)]
                    some = piece if some is None else some + piece
                some = some if par == e else swapped(some)
                value = some if value is None else value + some
            halves.append(value)
        kernels[pl.ds(pair * 64, 64), :] = jnp.where(low, halves[0], halves[1])

    per = mine.shape[0]
    n, r = lax.axis_index("narrow"), lax.axis_index("region")
    core, levels_z = lax.rem(r, 2), n_region // 2
    place = n * levels_z + r // 2
    per_core = core_sum.shape[0]

    def piece(o, size):
        return pl.ds(pl.multiple_of(o * size, size), size)

    to_core = pltpu.make_async_remote_copy(
        src_ref=kernels.at[piece(1 - core, per_core)],
        dst_ref=core_part,
        send_sem=core_send,
        recv_sem=core_recv,
        device_id=(n, r + 1 - 2 * core),
        device_id_type=MESH,
    )
    to_core.start()

    def emit(xp, total):
        t = total.T
        for i in range(2):
            at = pl.ds(pl.multiple_of((2 * xp + i) * 64, 64), 64)
            for m in range(2):
                a = t[i * 128 : i * 128 + 64, m * 128 : (m + 1) * 128]
                b = t[i * 128 + 64 : i * 128 + 128, m * 128 : (m + 1) * 128]
                planes[2 * m, at, :] = jnp.where(low, a, swapped(b))
                planes[2 * m + 1, at, :] = jnp.where(low, swapped(a), b)

    third = rows_x // 6
    convolve(stack, w, emit, 0, third)
    to_core.wait()
    core_sum[...] = kernels[piece(core, per_core), :] + core_part[...]
    parts_in = to_each(
        devices // 2,
        levels_z,
        place,
        lambda o: core_sum.at[piece(o, per)],
        parts.at[place],
        part_send,
        part_recv,
        where=lambda o, _: (o // levels_z, 2 * lax.rem(o, levels_z) + core),
    )
    parts[place] = core_sum[piece(place, per), :]
    convolve(stack, w, emit, third, rows_x // 2)

    def settle(o, _):
        for j in range(CY // 2):
            t = planes[j, pl.ds(o, rows_x, stride=outs), :]
            result[o, :, pl.ds(j * 128, 128)] = t.astype(bf16)

    lax.fori_loop(0, outs, settle, None)

    parts_in()
    total = lax.fori_loop(1, devices // 2, lambda s, total: total + parts[s], parts[0])
    mine[...] = (total * scale).astype(bf16)
    gathered = to_each(
        devices, n_region, me, lambda o: mine, sums.at[me], all_send, all_recv
    )
    sums[me] = mine[...]

    arrive()
    rows = devices * half

    def unpack(s, _):
        t = back[s].astype(f32)
        at = pl.multiple_of(s * half, half)
        rows_buf[pl.ds(at, half), :] = t
        rows_buf[pl.ds(rows + at, half), :] = swapped(t)

    lax.fori_loop(0, devices, unpack, None)
    few = out_buf.shape[0]
    points = point_out.shape[1]
    row_low = low_lanes(1)

    def gather(j, _):
        def group(g, _):
            for u in range(UNROLL):
                q = g * UNROLL + u
                a = rows_buf[pl.ds(collect[j * few + q], 1), :]
                b = rows_buf[pl.ds(collect[points // 2 + j * few + q], 1), :]
                out_buf[pl.ds(q, 1), :] = jnp.where(row_low, a, b)

        lax.fori_loop(0, few // UNROLL, group, None)
        t = out_buf[...].T.astype(bf16)
        at = pl.multiple_of(j * few, few)
        point_out[:, pl.ds(at, few)] = t[:64]
        point_out[:, pl.ds(points // 2 + at, few)] = t[64:]

    lax.fori_loop(0, points // 2 // few, gather, None)
    gathered()

    def widen_sums(s, _):
        at = lax.rem(s, 2) * per_core + s // 2 * per
        weight_out[pl.ds(pl.multiple_of(at, per), per), :] = sums[s].astype(f32)

    lax.fori_loop(0, devices, widen_sums, None)


def call(kernel, out_shape, kinds, out_kinds, scratch, collective_id, cost, *operands):
    where = {"s": pltpu.SMEM, "v": pltpu.VMEM, "a": pl.ANY}
    specs = [pl.BlockSpec(memory_space=where[k]) for k in out_kinds]
    remote = {} if collective_id is None else dict(collective_id=collective_id, has_side_effects=True)
    return pl.pallas_call(
        kernel,
        out_shape=out_shape,
        in_specs=[pl.BlockSpec(memory_space=where[k]) for k in kinds],
        out_specs=specs if len(specs) > 1 else specs[0],
        scratch_shapes=scratch,
        compiler_params=pltpu.CompilerParams(vmem_limit_bytes=56 << 20, **remote),
        cost_estimate=pl.CostEstimate(flops=0, bytes_accessed=cost, transcendentals=0),
    )(*operands)


def halo_scratch(rows_x):
    bf16 = jnp.bfloat16
    side = pltpu.VMEM((rows_x // 2, NZ, 128), bf16)
    end = pltpu.VMEM((PAIRS, NZ, 128), bf16)
    return [
        pltpu.VMEM((2, rows_x // 2, NZ, 128), bf16),
        side,
        side,
        end,
        end,
        pltpu.VMEM((4, NZ, 128), bf16),
        pltpu.VMEM((rows_x + 2, 3, PAIRS * NZ, 128), bf16),
    ]


def ranks(owner, devices):
    span = 128
    chunks = owner.shape[0] // span
    marks = owner.reshape(chunks, span)[:, :, None] == jnp.arange(devices, dtype=jnp.int32)
    ones = marks.astype(jnp.bfloat16)
    before = (jnp.arange(span)[:, None] > jnp.arange(span)[None, :]).astype(jnp.bfloat16)
    inner = jnp.einsum("ij,cjo->cio", before, ones, preferred_element_type=jnp.float32)
    tallies = jnp.sum(ones.astype(jnp.float32), axis=1)
    ahead = (jnp.arange(chunks)[:, None] > jnp.arange(chunks)[None, :]).astype(jnp.bfloat16)
    starts = jnp.einsum("ij,jo->io", ahead, tallies.astype(jnp.bfloat16), preferred_element_type=jnp.float32)
    slot = jnp.sum(jnp.where(marks, inner + starts[:, None, :], 0.0), axis=2)
    return slot.reshape(-1).astype(jnp.int32), jnp.sum(tallies, axis=0).astype(jnp.int32)


def shards(point_feats, point_owner, point_voxel, weight, cotangent):
    n_narrow = lax.axis_size("narrow")
    n_region = lax.axis_size("region")
    devices = n_narrow * n_region
    chans, points_here = point_feats.shape
    slots = 2 * points_here // devices
    half = slots // 2
    rows = devices * half
    rows_x = cotangent.shape[1]
    voxels = rows_x * CY * NZ
    f32, bf16, i32 = jnp.float32, jnp.bfloat16, jnp.int32
    dma = pltpu.SemaphoreType.DMA

    grads = cotangent.reshape(chans, rows_x, CY, NZ).transpose(1, 2, 3, 0)
    planes = pltpu.VMEM((CY // 2, rows_x * chans, 2 * NZ), f32)
    weights = pltpu.VMEM((5, 3, 4 * chans, 2 * chans), bf16)

    owner = point_owner[:, 0]
    slot, sent = ranks(owner, devices)
    marks = owner[:, None] == jnp.arange(devices, dtype=i32)
    index = jnp.arange(points_here, dtype=i32)
    values = jnp.stack([index // 64, index % 64, point_voxel // 128, point_voxel % 128], axis=1)
    named = jnp.where(marks[:, None, :], values[:, :, None], 0).astype(bf16).reshape(points_here, -1)
    seats = (slot[:, None] == jnp.arange(slots, dtype=i32)).astype(bf16)
    dealt = jnp.einsum("pa,ps->as", named, seats, preferred_element_type=f32)
    dealt = dealt.reshape(4, devices, slots)
    source = (dealt[0] * 64 + dealt[1]).astype(i32)
    filled = jnp.arange(slots, dtype=i32)[None, :] < sent[:, None]
    names = jnp.where(filled, (dealt[2] * 128 + dealt[3]).astype(i32), voxels)
    wide = -(-slots // 128) * 128
    names = jnp.pad(names, ((0, 0), (0, wide - slots))).reshape(devices, wide // 128, 128)
    feats = jnp.concatenate([point_feats, point_feats], axis=0).T.astype(f32)

    got, got_names, packed_table, turned = call(
        functools.partial(outward_kernel, n_narrow, n_region),
        (
            jax.ShapeDtypeStruct((devices, half, 2 * chans), bf16),
            jax.ShapeDtypeStruct(names.shape, i32),
            jax.ShapeDtypeStruct((voxels // 2, 2 * chans), bf16),
            jax.ShapeDtypeStruct((4 * chans, voxels // 4), bf16),
        ),
        "ssvvvva",
        "vvvv",
        [
            planes,
            pltpu.VMEM(cotangent.shape, bf16),
            dma,
            pltpu.VMEM((rows_x, PAIRS, NZ, 2 * chans), bf16),
            weights,
            pltpu.VMEM((devices, half, 2 * chans), bf16),
            pltpu.VMEM((half, 2 * chans), f32),
        ]
        + halo_scratch(rows_x)
        + [dma((devices,))] * 4
        + [dma((8,)), dma((8,))],
        0,
        60 << 20,
        source[:, :half].reshape(-1),
        source[:, half:].reshape(-1),
        feats,
        names,
        grads,
        weight,
        cotangent,
    )

    got_vox = got_names.reshape(devices, wide)[:, :slots]
    padded_y = got_vox // NZ % CY + 1
    row = (got_vox // (CY * NZ) * PAIRS + padded_y // 2) * NZ + got_vox % NZ
    there = got_vox < voxels
    add_at = jnp.where(there, row, rows_x * PAIRS * NZ)
    seats = jnp.arange(slots, dtype=i32)[None, :]
    form = 2 * (seats // half) + padded_y % 2
    add_from = form * rows + jnp.arange(devices, dtype=i32)[:, None] * half + seats % half
    pick_at = jnp.where(there, got_vox, 0)

    cells = call(
        functools.partial(splat_kernel, devices, slots),
        jax.ShapeDtypeStruct((rows_x, PAIRS, NZ, 2 * chans), bf16),
        "ssv",
        "v",
        [pltpu.VMEM((4 * rows, 2 * chans), f32)]
        + [pltpu.VMEM((rows_x * PAIRS * NZ + 8, 2 * chans), f32)] * COPIES,
        None,
        60 << 20,
        add_from.reshape(-1),
        add_at.reshape(-1),
        got,
    )

    seat = owner * half + slot % half
    side = slot // half
    wanted = index // (points_here // 2)
    collect = jnp.where(side == wanted, 0, rows) + seat
    total_cells = rows_x * n_region * CY * n_narrow * NZ
    kernel_rows = 1024
    per = kernel_rows // devices
    few = 128
    result, point_grad, kernels = call(
        functools.partial(inward_kernel, n_narrow, n_region, 1.0 / math.sqrt(total_cells)),
        (
            jax.ShapeDtypeStruct((chans, rows_x, CY * NZ), bf16),
            jax.ShapeDtypeStruct((chans, points_here), bf16),
            jax.ShapeDtypeStruct((kernel_rows, 2 * chans), f32),
        ),
        "sssvvvv",
        "vvv",
        [
            weights,
            planes,
            pltpu.VMEM((voxels, 2 * chans), f32),
            pltpu.VMEM((devices, half, 2 * chans), bf16),
            pltpu.VMEM((devices, half, 2 * chans), bf16),
            pltpu.VMEM((half, 2 * chans), f32),
        ]
        + halo_scratch(rows_x)
        + [
            pltpu.VMEM((12, 4 * chans, 4 * chans), f32),
            pltpu.VMEM((kernel_rows, 2 * chans), f32),
            pltpu.VMEM((kernel_rows // 2, 2 * chans), f32),
            pltpu.VMEM((kernel_rows // 2, 2 * chans), f32),
            pltpu.VMEM((devices // 2, per, 2 * chans), f32),
            pltpu.VMEM((per, 2 * chans), bf16),
            pltpu.VMEM((devices, per, 2 * chans), bf16),
            pltpu.VMEM((2 * rows, 2 * chans), f32),
            pltpu.VMEM((few, 2 * chans), f32),
        ]
        + [dma((devices,)), dma((devices,)), dma((8,)), dma((8,))]
        + [dma, dma, dma((devices // 2,)), dma((devices // 2,)), dma((devices,)), dma((devices,))],
        1,
        100 << 20,
        pick_at[:, :half].reshape(-1),
        pick_at[:, half:].reshape(-1),
        collect,
        packed_table,
        cells,
        turned,
        weight.transpose(0, 2, 1),
    )
    kernels = kernels.reshape(kernel_rows // 64, 64, 2, 64).transpose(0, 2, 1, 3).reshape(-1, 64, 64)
    weight_grad = kernels[:27].reshape(9, 3, 64, 64).transpose(0, 2, 1, 3).reshape(9, 64, 192)
    return (result, point_grad, weight_grad)


def solution(mesh):
    in_specs = (
        P(None, AXES),
        P(AXES, None),
        P(AXES),
        P(),
        P(None, "region", "narrow"),
    )
    out_specs = (P(None, "region", "narrow"), P(None, AXES), P())
    return jax.shard_map(shards, mesh=mesh, in_specs=in_specs, out_specs=out_specs, check_vma=False)
```

```python
import functools
import math

import jax
import jax.numpy as jnp
from jax import lax
from jax.experimental import pallas as pl
from jax.experimental.pallas import tpu as pltpu
from jax.sharding import PartitionSpec as P

NZ = 64
CY = 8
AXES = ("narrow", "region")
UNROLL = 32
COPIES = 4
VISITS = 128
STEP = 72
PAIRS = CY // 2 + 1
MESH = pl.DeviceIdType.MESH


def dot(a, b):
    return jnp.dot(a, b, preferred_element_type=jnp.float32)


def low_lanes(rows):
    return lax.broadcasted_iota(jnp.int32, (rows, 128), 1) < 64


def swapped(t):
    return pltpu.roll(t, 64, 1)


def device(flat, n_region):
    return (flat // n_region, lax.rem(flat, n_region))


def greet_all(devices, n_region, me):
    barrier = pltpu.get_barrier_semaphore()

    def greet(s, _):
        other = device(lax.rem(me + s, devices), n_region)
        pl.semaphore_signal(barrier, inc=1, device_id=other, device_id_type=MESH)

    lax.fori_loop(1, devices, greet, None)
    return lambda: pl.semaphore_wait(barrier, devices - 1)


def halo_moves(n_narrow, n_region, center, faces, left, right, top, bottom, corners, send, recv):
    n, r = lax.axis_index("narrow"), lax.axis_index("region")
    last = center.shape[0] - 1
    west, east = lax.rem(n + n_narrow - 1, n_narrow), lax.rem(n + 1, n_narrow)
    north, south = lax.rem(r + n_region - 1, n_region), lax.rem(r + 1, n_region)
    w, e, u, d = n > 0, n < n_narrow - 1, r > 0, r < n_region - 1
    both = jnp.logical_and
    table = [
        (w, e, (west, r), faces.at[0], right),
        (e, w, (east, r), faces.at[1], left),
        (u, d, (n, north), center.at[0], bottom),
        (d, u, (n, south), center.at[last], top),
        (both(w, u), both(e, d), (west, north), center.at[0, 0], corners.at[3]),
        (both(e, u), both(w, d), (east, north), center.at[0, PAIRS - 1], corners.at[2]),
        (both(w, d), both(e, u), (west, south), center.at[last, 0], corners.at[1]),
        (both(e, d), both(w, u), (east, south), center.at[last, PAIRS - 1], corners.at[0]),
    ]
    return [
        (
            sends,
            gets,
            pltpu.make_async_remote_copy(
                src_ref=source,
                dst_ref=target,
                send_sem=send.at[i],
                recv_sem=recv.at[i],
                device_id=where,
                device_id_type=MESH,
            ),
            target,
        )
        for i, (sends, gets, where, source, target) in enumerate(table)
    ]


def start_halo(moves, center, faces):
    half_x = center.shape[0] // 2
    f32 = jnp.float32

    def face(x, _):
        for i, k in ((0, 0), (1, PAIRS - 1)):
            tile = center[x, k].astype(f32) + swapped(center[x + half_x, k].astype(f32))
            faces[i, x] = tile.astype(jnp.bfloat16)

    lax.fori_loop(0, half_x, face, None)
    for sends, gets, copy, target in moves:

        @pl.when(sends)
        def _():
            copy.start()

        @pl.when(jnp.logical_not(gets))
        def _():
            target[...] = jnp.zeros(target.shape, target.dtype)


def wait_halo(moves):
    for sends, gets, copy, _ in moves:

        @pl.when(gets)
        def _():
            copy.wait_recv()

        @pl.when(sends)
        def _():
            copy.wait_send()


def put(stack, x, k, t):
    row = lax.broadcasted_iota(jnp.int32, t.shape, 0)
    at = pl.ds(k * NZ, NZ)
    up = jnp.where(row == 0, 0.0, pltpu.roll(t, 1, 0))
    down = jnp.where(row == NZ - 1, 0.0, pltpu.roll(t, NZ - 1, 0))
    stack[x, 0, at, :] = up.astype(jnp.bfloat16)
    stack[x, 1, at, :] = t.astype(jnp.bfloat16)
    stack[x, 2, at, :] = down.astype(jnp.bfloat16)


def stack_inside(stack, center):
    def plane(x, _):
        for k in range(1, PAIRS - 1):
            put(stack, x + 1, k, center[x, k].astype(jnp.float32))

    lax.fori_loop(0, center.shape[0], plane, None)


def stack_edges(stack, center, left, right, top, bottom, corners):
    rows_x = center.shape[0]
    half_x = rows_x // 2
    f32 = jnp.float32
    low = low_lanes(NZ)
    end = PAIRS - 1

    def sides(x, _):
        from_left, from_right = left[x].astype(f32), right[x].astype(f32)
        for at, l, r in (
            (x, from_left, from_right),
            (x + half_x, swapped(from_left), swapped(from_right)),
        ):
            put(stack, at + 1, 0, center[at, 0].astype(f32) + jnp.where(low, l, 0.0))
            put(stack, at + 1, end, center[at, end].astype(f32) + jnp.where(low, 0.0, r))

    lax.fori_loop(0, half_x, sides, None)
    for x, rows, c in ((0, top, 0), (rows_x + 1, bottom, 2)):
        for k in range(PAIRS):
            t = rows[k].astype(f32)
            if k == 0:
                t += corners[c].astype(f32)
            if k == end:
                t += corners[c + 1].astype(f32)
            put(stack, x, k, t)


def window(stack, x, d):
    rows = (PAIRS - 1) * NZ
    return jnp.concatenate([stack[x, d, pl.ds(0, rows), :], stack[x, d, pl.ds(NZ, rows), :]], axis=1)


def spread_weights(w, block):
    zero = jnp.zeros((64, 64), jnp.float32)
    for a in (0, 4):
        w[a] = jnp.zeros(w.shape[1:], w.dtype)
    for a in range(3):
        for d in range(3):
            for q in range(4):
                left = block(a, q, d) if q < 3 else zero
                right = block(a, q - 1, d) if q > 0 else zero
                both = jnp.concatenate([left, right], axis=1)
                w[a + 1, d, pl.ds(q * 64, 64), :] = both.astype(jnp.bfloat16)


def convolve(stack, w, emit, first, last):
    def step(xp, _):
        total = None
        for i in range(4):
            for d in range(3):
                both = jnp.concatenate([w[i + 1, d], w[i, d]], axis=1)
                term = dot(window(stack, 2 * xp + i, d), both)
                total = term if total is None else total + term
        emit(xp, total)

    lax.fori_loop(first, last, step, None)


def far_first(step, devices, n_region, me):
    n_narrow = devices // n_region
    turn = step // n_narrow
    off = n_region // 2 + (turn + 1) // 2 * (1 - 2 * lax.rem(turn, 2))
    n = lax.rem(me // n_region + lax.rem(step, n_narrow) + 1, n_narrow)
    return n * n_region + lax.rem(lax.rem(me, n_region) + off, n_region)


def to_each(devices, n_region, me, source, target, send, recv, visit=None, where=device):
    def copy(s):
        other = far_first(s, devices, n_region, me)
        return pltpu.make_async_remote_copy(
            src_ref=source(other),
            dst_ref=target,
            send_sem=send.at[s],
            recv_sem=recv.at[s],
            device_id=where(other, n_region),
            device_id_type=MESH,
        )

    def go(s, _):
        if visit is not None:
            visit(far_first(s, devices, n_region, me))
        copy(s).start()

    def finish(s, _):
        copy(s).wait_recv()
        copy(s).wait_send()

    lax.fori_loop(0, devices - 1, go, None)
    return lambda: lax.fori_loop(0, devices - 1, finish, None)


def paired_rows(first, second, table, base, rows, buf):
    low = low_lanes(1)

    def group(j, _):
        for u in range(UNROLL):
            q = j * UNROLL + u
            a = table[pl.ds(first[base + q], 1), :]
            b = table[pl.ds(second[base + q], 1), :]
            buf[pl.ds(q, 1), :] = jnp.where(low, a, b)

    lax.fori_loop(0, rows // UNROLL, group, None)


def outward_kernel(
    n_narrow, n_region, first, second, feats, names, grads, weight, far_cot,
    got, got_names, table, turned,
    planes, cot, cot_sem, center, w, block, buf, faces, left, right, top, bottom, corners, stack,
    send, recv, name_send, name_recv, halo_send, halo_recv,
):
    devices = n_narrow * n_region
    me = lax.axis_index("narrow") * n_region + lax.axis_index("region")
    half = buf.shape[0]
    f32 = jnp.float32
    bf16 = jnp.bfloat16
    fetch = pltpu.make_async_copy(far_cot, cot, cot_sem)
    fetch.start()
    met = greet_all(devices, n_region, me)
    zero = jnp.zeros((NZ, 64), f32)

    def pairs(x, _):
        for k in range(PAIRS):
            a = grads[x, 2 * k - 1].astype(f32) if k > 0 else zero
            b = grads[x, 2 * k].astype(f32) if k < PAIRS - 1 else zero
            center[x, k] = jnp.concatenate([a, b], axis=1).astype(jnp.bfloat16)

    lax.fori_loop(0, center.shape[0], pairs, None)
    met()
    moves = halo_moves(
        n_narrow, n_region, center, faces, left, right, top, bottom, corners, halo_send, halo_recv
    )
    start_halo(moves, center, faces)

    def fill(ref, at, other):
        paired_rows(first, second, feats, other * half, half, buf)
        ref[at] = buf[...].astype(jnp.bfloat16)

    arrive = to_each(
        devices, n_region, me, lambda o: block.at[o], got.at[me], send, recv, lambda o: fill(block, o, o)
    )
    named = to_each(
        devices, n_region, me, lambda o: names.at[o], got_names.at[me], name_send, name_recv
    )
    fill(got, me, me)
    got_names[me] = names[me]
    span = (PAIRS - 1) * NZ
    outs, rows_x = cot.shape[:2]
    low = low_lanes(NZ)
    fetch.wait()

    def lay(o, _):
        for j in range(CY // 2):
            t = cot[o, :, pl.ds(j * 128, 128)].astype(f32)
            planes[j, pl.ds(pl.multiple_of(o * rows_x, 8), rows_x), :] = t

    lax.fori_loop(0, outs, lay, None)

    def turn(xp, _):
        for i in range(2):
            some = pl.ds(2 * xp + i, outs, stride=rows_x)
            for m in range(2):
                a, b = planes[2 * m, some, :], planes[2 * m + 1, some, :]
                at = pl.ds(pl.multiple_of(xp * span + m * 128, 128), 128)
                turned[pl.ds(2 * i * 64, 64), at] = jnp.where(low, a, swapped(b)).astype(bf16)
                turned[pl.ds((2 * i + 1) * 64, 64), at] = jnp.where(low, swapped(a), b).astype(bf16)

    lax.fori_loop(0, rows_x // 2, turn, None)
    stack_inside(stack, center)
    wait_halo(moves)
    stack_edges(stack, center, left, right, top, bottom, corners)
    rows = (PAIRS - 1) * NZ
    spread_weights(
        w, lambda a, b, d: weight[8 - 3 * a - b, :, pl.ds(0, 192)].astype(f32)[:, 128 - d * 64 : 192 - d * 64]
    )

    def emit(xp, total):
        for i in range(2):
            at = pl.multiple_of((2 * xp + i) * rows, rows)
            table[pl.ds(at, rows), :] = total[:, i * 128 : (i + 1) * 128].astype(jnp.bfloat16)

    convolve(stack, w, emit, 0, rows_x // 2)
    arrive()
    named()


def splat_kernel(devices, slots, from_ref, to_ref, got_ref, cells_ref, buf, *sums):
    half = slots // 2
    rows = devices * half
    f32 = jnp.float32
    low = low_lanes(half)

    def load(s, _):
        t = got_ref[s].astype(f32)
        a, b = jnp.where(low, t, 0.0), jnp.where(low, 0.0, t)
        at = pl.multiple_of(s * half, half)
        for i, form in enumerate((a, swapped(a), swapped(b), b)):
            buf[pl.ds(i * rows + at, half), :] = form

    lax.fori_loop(0, devices, load, None)
    rows_x, pairs = cells_ref.shape[:2]
    span = pairs * NZ

    def clear(x, _):
        for each in sums:
            each[pl.ds(pl.multiple_of(x * span, span), span), :] = jnp.zeros((span, 128), f32)

    lax.fori_loop(0, rows_x, clear, None)

    def visits(j, _):
        for u in range(0, VISITS, len(sums)):
            k = j * VISITS + u
            at = [pl.ds(to_ref[k + i], 1) for i in range(len(sums))]
            new = [
                each[at[i], :] + buf[pl.ds(from_ref[k + i], 1), :] for i, each in enumerate(sums)
            ]
            for i, each in enumerate(sums):
                each[at[i], :] = new[i]

    lax.fori_loop(0, devices * slots // VISITS, visits, None)

    def finish(x, _):
        for k in range(pairs):
            at = pl.ds(pl.multiple_of(x * span + k * NZ, NZ), NZ)
            total = sums[0][at, :]
            for each in sums[1:]:
                total += each[at, :]
            cells_ref[x, k] = total.astype(jnp.bfloat16)

    lax.fori_loop(0, rows_x, finish, None)


def inward_kernel(
    n_narrow, n_region, scale, first, second, collect, packed_table, center, grads, weight,
    result, point_out, weight_out,
    w, planes, table, block, back, buf, faces, left, right, top, bottom, corners, stack,
    products, kernels, core_part, core_sum, parts, mine, sums, rows_buf, out_buf,
    send, recv, halo_send, halo_recv, core_send, core_recv, part_send, part_recv, all_send, all_recv,
):
    devices = n_narrow * n_region
    me = lax.axis_index("narrow") * n_region + lax.axis_index("region")
    half = buf.shape[0]
    f32, bf16 = jnp.float32, jnp.bfloat16
    low = low_lanes(NZ)
    rows_x = center.shape[0]
    met = greet_all(devices, n_region, me)
    met()
    moves = halo_moves(
        n_narrow, n_region, center, faces, left, right, top, bottom, corners, halo_send, halo_recv
    )
    start_halo(moves, center, faces)

    def widen(t, _):
        u = packed_table[pl.ds(pl.multiple_of(t * NZ, NZ), NZ), :].astype(f32)
        v = swapped(u)
        at = pl.multiple_of(t * 2 * NZ, 2 * NZ)
        table[pl.ds(at, NZ), :] = jnp.where(low, u, v)
        table[pl.ds(at + NZ, NZ), :] = jnp.where(low, v, u)

    lax.fori_loop(0, packed_table.shape[0] // NZ, widen, None)

    def fill(ref, at, other):
        paired_rows(first, second, table, other * half, half, buf)
        ref[at] = buf[...].astype(bf16)

    arrive = to_each(
        devices, n_region, me, lambda o: block.at[o], back.at[me], send, recv, lambda o: fill(block, o, o)
    )
    fill(back, me, me)
    span = (PAIRS - 1) * NZ
    outs = weight.shape[2]
    stack_inside(stack, center)
    wait_halo(moves)
    stack_edges(stack, center, left, right, top, bottom, corners)

    def product(t, _):
        total = None
        for xp in range(rows_x // 2):
            here = grads[:, pl.ds(xp * span, span)]
            term = dot(here, window(stack, 2 * xp + t // 3, lax.rem(t, 3)))
            total = term if total is None else total + term
        products[t] = total

    lax.fori_loop(0, 12, product, None)

    kernels[...] = jnp.zeros_like(kernels)
    for pair in range(14):
        halves = []
        for e in range(2):
            t = 2 * pair + e
            if t >= 27:
                halves.append(jnp.zeros((64, 128), f32))
                continue
            a, b, d = t // 9, t // 3 % 3, t % 3
            value = None
            for p in range(2):
                q = b + p
                m, par = q // 2, q % 2
                some = None
                for i in range(2):
                    piece = products[(a + i) * 3 + d, pl.ds((2 * i + p) * 64, 64), pl.ds(m * 128, 128)]
                    some = piece if some is None else some + piece
                some = some if par == e else swapped(some)
                value = some if value is None else value + some
            halves.append(value)
        kernels[pl.ds(pair * 64, 64), :] = jnp.where(low, halves[0], halves[1])

    per = mine.shape[0]
    n, r = lax.axis_index("narrow"), lax.axis_index("region")
    core, levels_z = lax.rem(r, 2), n_region // 2
    place = n * levels_z + r // 2
    per_core = core_sum.shape[0]

    def piece(o, size):
        return pl.ds(pl.multiple_of(o * size, size), size)

    to_core = pltpu.make_async_remote_copy(
        src_ref=kernels.at[piece(1 - core, per_core)],
        dst_ref=core_part,
        send_sem=core_send,
        recv_sem=core_recv,
        device_id=(n, r + 1 - 2 * core),
        device_id_type=MESH,
    )
    to_core.start()
    spread_weights(w, lambda a, b, d: weight[3 * a + b, pl.ds(d * 64, 64), :].astype(f32))

    def emit(xp, total):
        t = total.T
        for i in range(2):
            at = pl.ds(pl.multiple_of((2 * xp + i) * STEP, 8), 64)
            for m in range(2):
                a = t[i * 128 : i * 128 + 64, m * 128 : (m + 1) * 128]
                b = t[i * 128 + 64 : i * 128 + 128, m * 128 : (m + 1) * 128]
                planes[2 * m, at, :] = jnp.where(low, a, swapped(b))
                planes[2 * m + 1, at, :] = jnp.where(low, swapped(a), b)

    third = rows_x // 12
    convolve(stack, w, emit, 0, third)
    to_core.wait()
    core_sum[...] = kernels[piece(core, per_core), :] + core_part[...]
    parts_in = to_each(
        devices // 2,
        levels_z,
        place,
        lambda o: core_sum.at[piece(o, per)],
        parts.at[place],
        part_send,
        part_recv,
        where=lambda o, _: (o // levels_z, 2 * lax.rem(o, levels_z) + core),
    )
    parts[place] = core_sum[piece(place, per), :]
    convolve(stack, w, emit, third, rows_x // 2)

    def settle(o, _):
        for j in range(CY // 2):
            t = planes[j, pl.ds(o, rows_x, stride=STEP), :]
            result[o, :, pl.ds(j * 128, 128)] = t.astype(bf16)

    lax.fori_loop(0, outs, settle, None)

    parts_in()
    total = lax.fori_loop(1, devices // 2, lambda s, total: total + parts[s], parts[0])
    mine[...] = (total * scale).astype(bf16)
    gathered = to_each(
        devices, n_region, me, lambda o: mine, sums.at[me], all_send, all_recv
    )
    sums[me] = mine[...]

    arrive()
    rows = devices * half

    def unpack(s, _):
        t = back[s].astype(f32)
        at = pl.multiple_of(s * half, half)
        rows_buf[pl.ds(at, half), :] = t
        rows_buf[pl.ds(rows + at, half), :] = swapped(t)

    lax.fori_loop(0, devices, unpack, None)
    few = out_buf.shape[0]
    points = point_out.shape[1]
    row_low = low_lanes(1)

    def gather(j, _):
        def group(g, _):
            for u in range(UNROLL):
                q = g * UNROLL + u
                a = rows_buf[pl.ds(collect[j * few + q], 1), :]
                b = rows_buf[pl.ds(collect[points // 2 + j * few + q], 1), :]
                out_buf[pl.ds(q, 1), :] = jnp.where(row_low, a, b)

        lax.fori_loop(0, few // UNROLL, group, None)
        t = out_buf[...].T.astype(bf16)
        at = pl.multiple_of(j * few, few)
        point_out[:, pl.ds(at, few)] = t[:64]
        point_out[:, pl.ds(points // 2 + at, few)] = t[64:]

    lax.fori_loop(0, points // 2 // few, gather, None)
    gathered()

    def widen_sums(s, _):
        at = lax.rem(s, 2) * per_core + s // 2 * per
        weight_out[pl.ds(pl.multiple_of(at, per), per), :] = sums[s].astype(f32)

    lax.fori_loop(0, devices, widen_sums, None)


def call(kernel, out_shape, kinds, out_kinds, scratch, collective_id, cost, *operands):
    where = {"s": pltpu.SMEM, "v": pltpu.VMEM, "a": pl.ANY}
    specs = [pl.BlockSpec(memory_space=where[k]) for k in out_kinds]
    remote = {} if collective_id is None else dict(collective_id=collective_id, has_side_effects=True)
    return pl.pallas_call(
        kernel,
        out_shape=out_shape,
        in_specs=[pl.BlockSpec(memory_space=where[k]) for k in kinds],
        out_specs=specs if len(specs) > 1 else specs[0],
        scratch_shapes=scratch,
        compiler_params=pltpu.CompilerParams(vmem_limit_bytes=56 << 20, **remote),
        cost_estimate=pl.CostEstimate(flops=0, bytes_accessed=cost, transcendentals=0),
    )(*operands)


def halo_scratch(rows_x):
    bf16 = jnp.bfloat16
    side = pltpu.VMEM((rows_x // 2, NZ, 128), bf16)
    end = pltpu.VMEM((PAIRS, NZ, 128), bf16)
    return [
        pltpu.VMEM((2, rows_x // 2, NZ, 128), bf16),
        side,
        side,
        end,
        end,
        pltpu.VMEM((4, NZ, 128), bf16),
        pltpu.VMEM((rows_x + 2, 3, PAIRS * NZ, 128), bf16),
    ]


def ranks(owner, devices):
    span = 128
    chunks = owner.shape[0] // span
    marks = owner.reshape(chunks, span)[:, :, None] == jnp.arange(devices, dtype=jnp.int32)
    ones = marks.astype(jnp.bfloat16)
    before = (jnp.arange(span)[:, None] > jnp.arange(span)[None, :]).astype(jnp.bfloat16)
    inner = jnp.einsum("ij,cjo->cio", before, ones, preferred_element_type=jnp.float32)
    tallies = jnp.sum(ones.astype(jnp.float32), axis=1)
    ahead = (jnp.arange(chunks)[:, None] > jnp.arange(chunks)[None, :]).astype(jnp.bfloat16)
    starts = jnp.einsum("ij,jo->io", ahead, tallies.astype(jnp.bfloat16), preferred_element_type=jnp.float32)
    slot = jnp.sum(jnp.where(marks, inner + starts[:, None, :], 0.0), axis=2)
    return slot.reshape(-1).astype(jnp.int32), jnp.sum(tallies, axis=0).astype(jnp.int32)


def shards(point_feats, point_owner, point_voxel, weight, cotangent):
    n_narrow = lax.axis_size("narrow")
    n_region = lax.axis_size("region")
    devices = n_narrow * n_region
    chans, points_here = point_feats.shape
    slots = 2 * points_here // devices
    half = slots // 2
    rows = devices * half
    rows_x = cotangent.shape[1]
    voxels = rows_x * CY * NZ
    f32, bf16, i32 = jnp.float32, jnp.bfloat16, jnp.int32
    dma = pltpu.SemaphoreType.DMA

    grads = cotangent.reshape(chans, rows_x, CY, NZ).transpose(1, 2, 3, 0)
    planes = pltpu.VMEM((CY // 2, rows_x * chans, 2 * NZ), f32)
    weights = pltpu.VMEM((5, 3, 4 * chans, 2 * chans), bf16)

    owner = point_owner[:, 0]
    slot, sent = ranks(owner, devices)
    marks = owner[:, None] == jnp.arange(devices, dtype=i32)
    index = jnp.arange(points_here, dtype=i32)
    values = jnp.stack([index // 64, index % 64, point_voxel // 128, point_voxel % 128], axis=1)
    named = jnp.where(marks[:, None, :], values[:, :, None], 0).astype(bf16).reshape(points_here, -1)
    seats = (slot[:, None] == jnp.arange(slots, dtype=i32)).astype(bf16)
    dealt = jnp.einsum("pa,ps->as", named, seats, preferred_element_type=f32)
    dealt = dealt.reshape(4, devices, slots)
    source = (dealt[0] * 64 + dealt[1]).astype(i32)
    filled = jnp.arange(slots, dtype=i32)[None, :] < sent[:, None]
    names = jnp.where(filled, (dealt[2] * 128 + dealt[3]).astype(i32), voxels)
    wide = -(-slots // 128) * 128
    names = jnp.pad(names, ((0, 0), (0, wide - slots))).reshape(devices, wide // 128, 128)
    feats = jnp.concatenate([point_feats, point_feats], axis=0).T.astype(f32)

    got, got_names, packed_table, turned = call(
        functools.partial(outward_kernel, n_narrow, n_region),
        (
            jax.ShapeDtypeStruct((devices, half, 2 * chans), bf16),
            jax.ShapeDtypeStruct(names.shape, i32),
            jax.ShapeDtypeStruct((voxels // 2, 2 * chans), bf16),
            jax.ShapeDtypeStruct((4 * chans, voxels // 4), bf16),
        ),
        "ssvvvva",
        "vvvv",
        [
            planes,
            pltpu.VMEM(cotangent.shape, bf16),
            dma,
            pltpu.VMEM((rows_x, PAIRS, NZ, 2 * chans), bf16),
            weights,
            pltpu.VMEM((devices, half, 2 * chans), bf16),
            pltpu.VMEM((half, 2 * chans), f32),
        ]
        + halo_scratch(rows_x)
        + [dma((devices,))] * 4
        + [dma((8,)), dma((8,))],
        0,
        60 << 20,
        source[:, :half].reshape(-1),
        source[:, half:].reshape(-1),
        feats,
        names,
        grads,
        weight,
        cotangent,
    )

    got_vox = got_names.reshape(devices, wide)[:, :slots]
    padded_y = got_vox // NZ % CY + 1
    row = (got_vox // (CY * NZ) * PAIRS + padded_y // 2) * NZ + got_vox % NZ
    there = got_vox < voxels
    add_at = jnp.where(there, row, rows_x * PAIRS * NZ)
    seats = jnp.arange(slots, dtype=i32)[None, :]
    form = 2 * (seats // half) + padded_y % 2
    add_from = form * rows + jnp.arange(devices, dtype=i32)[:, None] * half + seats % half
    pick_at = jnp.where(there, got_vox, 0)

    cells = call(
        functools.partial(splat_kernel, devices, slots),
        jax.ShapeDtypeStruct((rows_x, PAIRS, NZ, 2 * chans), bf16),
        "ssv",
        "v",
        [pltpu.VMEM((4 * rows, 2 * chans), f32)]
        + [pltpu.VMEM((rows_x * PAIRS * NZ + 8, 2 * chans), f32)] * COPIES,
        None,
        60 << 20,
        add_from.reshape(-1),
        add_at.reshape(-1),
        got,
    )

    seat = owner * half + slot % half
    side = slot // half
    wanted = index // (points_here // 2)
    collect = jnp.where(side == wanted, 0, rows) + seat
    total_cells = rows_x * n_region * CY * n_narrow * NZ
    kernel_rows = 1024
    per = kernel_rows // devices
    few = 128
    result, point_grad, kernels = call(
        functools.partial(inward_kernel, n_narrow, n_region, 1.0 / math.sqrt(total_cells)),
        (
            jax.ShapeDtypeStruct((chans, rows_x, CY * NZ), bf16),
            jax.ShapeDtypeStruct((chans, points_here), bf16),
            jax.ShapeDtypeStruct((kernel_rows, 2 * chans), f32),
        ),
        "sssvvvv",
        "vvv",
        [
            weights,
            pltpu.VMEM((CY // 2, rows_x * STEP, 2 * NZ), f32),
            pltpu.VMEM((voxels, 2 * chans), f32),
            pltpu.VMEM((devices, half, 2 * chans), bf16),
            pltpu.VMEM((devices, half, 2 * chans), bf16),
            pltpu.VMEM((half, 2 * chans), f32),
        ]
        + halo_scratch(rows_x)
        + [
            pltpu.VMEM((12, 4 * chans, 4 * chans), f32),
            pltpu.VMEM((kernel_rows, 2 * chans), f32),
            pltpu.VMEM((kernel_rows // 2, 2 * chans), f32),
            pltpu.VMEM((kernel_rows // 2, 2 * chans), f32),
            pltpu.VMEM((devices // 2, per, 2 * chans), f32),
            pltpu.VMEM((per, 2 * chans), bf16),
            pltpu.VMEM((devices, per, 2 * chans), bf16),
            pltpu.VMEM((2 * rows, 2 * chans), f32),
            pltpu.VMEM((few, 2 * chans), f32),
        ]
        + [dma((devices,)), dma((devices,)), dma((8,)), dma((8,))]
        + [dma, dma, dma((devices // 2,)), dma((devices // 2,)), dma((devices,)), dma((devices,))],
        1,
        100 << 20,
        pick_at[:, :half].reshape(-1),
        pick_at[:, half:].reshape(-1),
        collect,
        packed_table,
        cells,
        turned,
        weight.transpose(0, 2, 1),
    )
    kernels = kernels.reshape(kernel_rows // 64, 64, 2, 64).transpose(0, 2, 1, 3).reshape(-1, 64, 64)
    weight_grad = kernels[:27].reshape(9, 3, 64, 64).transpose(0, 2, 1, 3).reshape(9, 64, 192)
    return (result, point_grad, weight_grad)


def solution(mesh):
    in_specs = (
        P(None, AXES),
        P(AXES, None),
        P(AXES),
        P(),
        P(None, "region", "narrow"),
    )
    out_specs = (P(None, "region", "narrow"), P(None, AXES), P())
    return jax.shard_map(shards, mesh=mesh, in_specs=in_specs, out_specs=out_specs, check_vma=False)
```
